768 devices in a mesh: clu: 96 (over y, z), sub: 8 (over x, core).
Axes of the slice: x: 4, y: 8, z: 12, core: 2. Of those that a mesh axis runs over, the one named last changes fastest.
Arguments:
- operator: bfloat16 [768, 1024, 1024], P(('clu', 'sub')), as said below
- rhs: float32 [768, 1024, 128], P(('clu', 'sub')), may hold values from -6 to 6
- interface_sizes: int32 [768], P(('clu', 'sub')), may hold values from 64 to 1024, as said below
- neighbour_rows: int32 [768, 1024], P(('clu', 'sub')), may hold values from 0 to 1023, each once within a row
- kept_columns: int32 [1, 128], replicated, may hold values 0 or 1
Outputs:
- solution: float32 [768, 1024, 128], P(('clu', 'sub'))
- residual: float32 [768, 1024, 128], P(('clu', 'sub'))
- direction: float32 [768, 1024, 128], P(('clu', 'sub'))
The draws below stay inside these ranges and needn't reach their ends.
Inputs may be any that keep to these rules, and one draw needn't show every extreme that they name: `operator`: each subdomain's block is symmetric positive definite. `interface_sizes`: some subdomain has all 1024 multipliers live in every draw. `neighbour_rows`: each row is a permutation of 0 to 1023.
All inputs are finite; a program needn't handle non-finite values.
Results may differ from the reference program's by a relative error of at most 0.0065.
Values may be sent and summed in bfloat16 or wider, within the bound.
A program may use at most 32 MiB of HBM per device.

```python
import math
import jax
import jax.numpy as jnp
from jax import lax

MULT = 1024
DIRS = 128
ITERS = 1
SUBS = 768
N_CLU = 96
N_SUB = 8


def draw_operator(key, part):

    def single(subdomain):
        folded = jax.random.fold_in(key, subdomain)
        subkeys = jax.random.split(folded, 2)
        entries = jax.random.normal(subkeys[0], (MULT, MULT), jnp.float32)
        symmetric = (entries + entries.T) * (0.5 * MULT ** (-0.5))
        diagonal = 2.0 * jnp.exp(jax.random.uniform(subkeys[1], (MULT,), jnp.float32) * math.log(3.0))
        return (symmetric + jnp.diag(diagonal)).astype(jnp.bfloat16)
    return lax.map(single, jnp.arange(SUBS))


def draw_interface_sizes(key, part):
    first, second, third = jax.random.split(jax.random.fold_in(key, 17), 3)
    base = jax.random.randint(first, (SUBS,), MULT // 16, MULT // 8 + 1)
    power = jax.random.randint(second, (SUBS,), 0, 4)
    sizes = jnp.minimum(MULT, jnp.left_shift(base, power))
    chosen = jax.random.randint(third, (), 0, SUBS)
    return jnp.where(jnp.arange(SUBS) == chosen, MULT, sizes).astype(jnp.int32)


def touch_ends(values, rng, least, high):
    extent = values.shape
    place = [jax.random.randint(jax.random.fold_in(rng, axis), (), 0, extent[axis]) for axis in range(len(extent))]
    values = values.at[tuple(place)].set(least)
    longest = extent.index(max(extent))
    place[longest] = (place[longest] + 1) % extent[longest]
    return values.at[tuple(place)].set(high)


def steps_of(own_key, shape, cuts, low, high):
    gain = 1.0
    for dim, blocks in cuts:
        heights = jax.random.uniform(jax.random.fold_in(jax.random.fold_in(own_key, 6), dim), (blocks,), jnp.float32, low / len(cuts), high / len(cuts))
        gain = gain * jnp.repeat(jnp.exp(heights), shape[dim] // blocks).reshape((-1,) + (1,) * (len(shape) - 1 - dim))
    return gain


def scatter_about(stream_key, extent, spread, bound, shards=(), dtype=jnp.bfloat16):
    level = steps_of(stream_key, extent, shards, -0.22, 0.18) if shards else 1.0
    array = jax.random.normal(stream_key, extent, jnp.float32) * spread * level
    return jnp.minimum(jnp.maximum(array, -bound), bound).astype(dtype)


def setup_inputs(seed: int = 0) -> dict:
    splits = jax.random.split(jax.random.key(seed), 6)
    return {
        "operator": draw_operator(jax.random.fold_in(splits[5], 71), 0),
        "rhs": scatter_about(splits[1], (SUBS, MULT, DIRS), 1.0, 6.0, ((0, 768),), jnp.float32),
        "interface_sizes": draw_interface_sizes(jax.random.fold_in(splits[5], 71), 0),
        "neighbour_rows": jax.vmap(lambda own: jax.random.permutation(own, MULT))(jax.random.split(splits[3], SUBS)).reshape((SUBS, MULT)).astype(jnp.int32),
        "kept_columns": touch_ends((jax.random.randint(splits[4], (ITERS, DIRS), 0, 4) < 3).astype(jnp.int32), jax.random.fold_in(splits[4], 1), 0, 1),
    }


stiffness = 1.0

def apply_operator(operator, rounded, neighbour_rows, inverse, degree, rowmask):
    product = lax.map(lambda operands: jnp.dot(operands[0].astype(jnp.float32), operands[1].astype(jnp.float32), preferred_element_type=jnp.float32), (operator, rounded))
    grid = rounded.reshape(N_CLU, N_SUB, MULT, DIRS)
    ahead = jnp.take_along_axis(rounded, inverse[:, :, None], axis=1).reshape(N_CLU, N_SUB, MULT, DIRS)
    empty = jnp.zeros_like(grid[:1])
    behind = jnp.concatenate([empty, grid[:-1]], 0).reshape(SUBS, MULT, DIRS)
    left_rows = jnp.take_along_axis(behind, neighbour_rows[:, :, None], axis=1)
    right_rows = jnp.concatenate([ahead[1:], empty], 0).reshape(SUBS, MULT, DIRS)
    coupling = degree * rounded.astype(jnp.float32) - left_rows.astype(jnp.float32) - right_rows.astype(jnp.float32)
    return rowmask * (product + stiffness * coupling)

def reference(operator, rhs, interface_sizes, neighbour_rows, kept_columns):
    highest = lax.Precision.HIGHEST
    rowmask = (jnp.arange(MULT)[None, :] < interface_sizes[:, None]).astype(jnp.float32)[:, :, None]
    inverse = jnp.argsort(neighbour_rows, axis=1)
    position = jnp.arange(SUBS) // N_SUB
    degree = ((position > 0).astype(jnp.float32) + (position < N_CLU - 1).astype(jnp.float32))[:, None, None]
    residual = rhs * rowmask
    solution = jnp.zeros_like(residual)
    direction = residual
    for iteration in range(ITERS):
        keep = kept_columns[iteration].astype(jnp.float32)
        rounded = (direction * keep[None, None, :]).astype(jnp.bfloat16)
        image = apply_operator(operator, rounded, neighbour_rows, inverse, degree, rowmask)
        widened = rounded.astype(jnp.float32)
        curvature = jnp.einsum('smk,sml->kl', widened, image, precision=highest)
        projected = jnp.einsum('smk,sml->kl', widened, residual, precision=highest)
        regular = curvature + jnp.diag(1.0 - keep)
        factor = jnp.linalg.cholesky(regular)
        weights = jax.scipy.linalg.cho_solve((factor, True), projected)
        solution = solution + jnp.einsum('smk,kl->sml', widened, weights, precision=highest)
        residual = residual - jnp.einsum('smk,kl->sml', image, weights, precision=highest)
        coupled = jnp.einsum('smk,sml->kl', image, residual, precision=highest)
        correction = jax.scipy.linalg.cho_solve((factor, True), coupled)
        direction = residual - jnp.einsum('smk,kl->sml', widened, correction, precision=highest)
    return (solution, residual, direction)
```

```python
import functools

import jax
import jax.numpy as jnp
from jax import lax
from jax.experimental import pallas as pl
from jax.experimental.pallas import tpu as pltpu
from jax.sharding import Mesh
from jax.sharding import PartitionSpec as P

AXES = ("y", "z", "x", "core")
F32 = jnp.float32
BF16 = jnp.bfloat16
HIGHEST = lax.Precision.HIGHEST
CHUNKS = 4
stiffness = 1.0


def dot(a, b, contract=((1,), (0,)), precision=None):
    return lax.dot_general(a, b, (contract, ((), ())), precision=precision, preferred_element_type=F32)


def comm_kernel(
    ny, nz, nx, nc,
    op_hbm, rhs_ref, size_ref, nbr_ref, keep_ref,
    image_ref, sums_ref,
    op_ref, pt_ref, rounded_ref, ahead_ref, behind_ref, right_ref,
    gram_ref, xin_ref, ychunk_ref, yin_ref, zown_ref, zin_ref, part_ref,
    op_sem, f_send, f_recv, b_send, b_recv,
    xs, xr, ys, yr, zs, zr, ys2, yr2, xs2, xr2,
):
    y, z, x, core = (lax.axis_index(a) for a in AXES)
    clu = y * nz + z
    nclu = ny * nz
    nsub = nx * nc
    sub = x * nc + core
    nxt = lax.rem(clu + 1, nclu)
    prv = lax.rem(clu + nclu - 1, nclu)

    def at_clu(c):
        return (c // nz, lax.rem(c, nz), x, core)

    def at_sub(s):
        return (y, z, s // nc, lax.rem(s, nc))

    def at_y(v):
        return (v, z, x, core)

    def at_z(v):
        return (y, v, x, core)

    next_id, prev_id = at_clu(nxt), at_clu(prv)
    sub_ids = [None] + [at_sub(lax.rem(sub + d, nsub)) for d in range(1, nsub)]
    y_ids = [None] + [at_y(lax.rem(y + d, ny)) for d in range(1, ny)]
    z_ids = [None] + [at_z(lax.rem(z + d, nz)) for d in range(1, nz)]

    op_copy = pltpu.make_async_copy(op_hbm.at[0], op_ref, op_sem)
    op_copy.start()

    barrier = pltpu.get_barrier_semaphore()
    greeted = [next_id, prev_id] + sub_ids[1:] + y_ids[1:] + z_ids[1:]
    for device in greeted:
        pl.semaphore_signal(barrier, inc=1, device_id=device, device_id_type=pl.DeviceIdType.MESH)

    height, breadth = rounded_ref.shape
    step = height // CHUNKS
    size = size_ref[0]
    keep = keep_ref[...].astype(F32)

    def masked(t):
        rows = lax.broadcasted_iota(jnp.int32, (step, breadth), 0) + t * step
        return jnp.where(rows < size, rhs_ref[0, pl.ds(t * step, step), :], 0.0), rows

    for t in range(CHUNKS):
        live, _ = masked(t)
        rounded_ref[pl.ds(t * step, step), :] = (live * keep).astype(BF16)
        rows = lax.broadcasted_iota(jnp.int32, (step, height), 0) + t * step
        pt_ref[pl.ds(t * step, step), :] = jnp.where(rows == nbr_ref[...], 1.0, 0.0).astype(BF16)
    for t in range(CHUNKS):
        ahead_ref[pl.ds(t * step, step), :] = dot(pt_ref[pl.ds(t * step, step), :], rounded_ref[...]).astype(BF16)

    def remote(src, dst, send, recv, device):
        return pltpu.make_async_remote_copy(
            src_ref=src, dst_ref=dst, send_sem=send, recv_sem=recv,
            device_id=device, device_id_type=pl.DeviceIdType.MESH,
        )

    pl.semaphore_wait(barrier, len(greeted))

    forward, backward = [], []
    for t in range(CHUNKS):
        rows = pl.ds(t * step, step)
        forward.append(remote(rounded_ref.at[rows, :], behind_ref.at[rows, :], f_send.at[t], f_recv.at[t], next_id))
        backward.append(remote(ahead_ref.at[rows, :], right_ref.at[rows, :], b_send.at[t], b_recv.at[t], prev_id))
        forward[t].start()
        backward[t].start()

    has_prev = clu > 0
    has_next = clu < nclu - 1
    degree = has_prev.astype(F32) + has_next.astype(F32)
    op_copy.wait()
    for t in range(CHUNKS):
        rows = pl.ds(t * step, step)
        product = dot(op_ref[rows, :], rounded_ref[...])
        image_ref[rows, :] = product + stiffness * degree * rounded_ref[rows, :].astype(F32)

    prev_scale = jnp.where(has_prev, stiffness, 0.0).astype(F32)
    next_scale = jnp.where(has_next, stiffness, 0.0).astype(F32)
    left_t = None
    for t in range(CHUNKS):
        rows = pl.ds(t * step, step)
        forward[t].wait_recv()
        term = dot(behind_ref[rows, :].astype(F32).T.astype(BF16), pt_ref[rows, :])
        left_t = term if left_t is None else left_t + term
    left = left_t.T
    for t in range(CHUNKS):
        rows = pl.ds(t * step, step)
        backward[t].wait_recv()
        coupled = prev_scale * left[t * step : (t + 1) * step, :] + next_scale * right_ref[rows, :].astype(F32)
        live = lax.broadcasted_iota(jnp.int32, (step, breadth), 0) + t * step < size
        image_ref[rows, :] = jnp.where(live, image_ref[rows, :] - coupled, 0.0)

    gram = None
    for t in range(CHUNKS):
        rows = pl.ds(t * step, step)
        live, _ = masked(t)
        image = image_ref[rows, :]
        lhs = jnp.concatenate([rounded_ref[rows, :].astype(F32), image], axis=1)
        rhs = jnp.concatenate([image, live], axis=1)
        term = dot(lhs, rhs, ((0,), (0,)), HIGHEST)
        gram = term if gram is None else gram + term
    pieces = (
        gram[:breadth, :breadth], gram[:breadth, breadth:],
        gram[breadth:, :breadth], gram[breadth:, breadth:],
    )
    slab = breadth // nsub
    for s in range(nsub):
        for k, piece in enumerate(pieces):
            gram_ref[s, k * slab : (k + 1) * slab, :] = piece[s * slab : (s + 1) * slab, :]

    copies = []
    for d in range(1, nsub):
        peer = lax.rem(sub + d, nsub)
        copies.append(remote(gram_ref.at[peer], xin_ref.at[d], xs.at[d], xr.at[d], sub_ids[d]))
        copies[-1].start()
    total = gram_ref[sub]
    for d in range(1, nsub):
        copies[d - 1].wait_recv()
        total = total + xin_ref[d]
    height_y = total.shape[0] // ny
    for v in range(ny):
        ychunk_ref[v] = total[v * height_y : (v + 1) * height_y, :]

    ycopies = []
    for d in range(1, ny):
        peer = lax.rem(y + d, ny)
        ycopies.append(remote(ychunk_ref.at[peer], yin_ref.at[d], ys.at[d], yr.at[d], y_ids[d]))
        ycopies[-1].start()
    total = ychunk_ref[y]
    for d in range(1, ny):
        ycopies[d - 1].wait_recv()
        total = total + yin_ref[d]
    zown_ref[...] = total

    zcopies = []
    for d in range(1, nz):
        zcopies.append(remote(zown_ref, zin_ref.at[d], zs.at[d], zr.at[d], z_ids[d]))
        zcopies[-1].start()
    for d in range(1, nz):
        zcopies[d - 1].wait_recv()
        total = total + zin_ref[d]
    part_ref[y] = total

    y2 = []
    for d in range(1, ny):
        y2.append(remote(part_ref.at[y], part_ref.at[y], ys2.at[d], yr2.at[d], y_ids[d]))
        y2[-1].start()
    for d in range(1, ny):
        y2[d - 1].wait_recv()
    for v in range(ny):
        sums_ref[sub, v * height_y : (v + 1) * height_y, :] = part_ref[v]
    x2 = []
    for d in range(1, nsub):
        x2.append(remote(sums_ref.at[sub], sums_ref.at[sub], xs2.at[d], xr2.at[d], sub_ids[d]))
        x2[-1].start()
    for d in range(1, nsub):
        x2[d - 1].wait_recv()
    for copy in forward + backward + copies + ycopies + zcopies + y2 + x2:
        copy.wait_send()


def communicate(operator, rhs, sizes, neighbours, kept, ny, nz, nx, nc):
    height, breadth = rhs.shape[1:]
    nsub = nx * nc
    slab = 4 * breadth // nsub
    piece = slab // ny
    vmem = pl.BlockSpec(memory_space=pltpu.VMEM)
    dma = pltpu.SemaphoreType.DMA
    return pl.pallas_call(
        functools.partial(comm_kernel, ny, nz, nx, nc),
        name="exchange_and_sums",
        out_shape=(
            jax.ShapeDtypeStruct((height, breadth), F32),
            jax.ShapeDtypeStruct((nsub, slab, breadth), F32),
        ),
        in_specs=[
            pl.BlockSpec(memory_space=pl.ANY), vmem, pl.BlockSpec(memory_space=pltpu.SMEM), vmem, vmem,
        ],
        out_specs=(vmem, vmem),
        scratch_shapes=[
            pltpu.VMEM((height, height), BF16),
            pltpu.VMEM((height, height), BF16),
            pltpu.VMEM((height, breadth), BF16),
            pltpu.VMEM((height, breadth), BF16),
            pltpu.VMEM((height, breadth), BF16),
            pltpu.VMEM((height, breadth), BF16),
            pltpu.VMEM((nsub, slab, breadth), F32),
            pltpu.VMEM((nsub, slab, breadth), F32),
            pltpu.VMEM((ny, piece, breadth), F32),
            pltpu.VMEM((ny, piece, breadth), F32),
            pltpu.VMEM((piece, breadth), F32),
            pltpu.VMEM((nz, piece, breadth), F32),
            pltpu.VMEM((ny, piece, breadth), F32),
            dma(()),
            dma((CHUNKS,)), dma((CHUNKS,)), dma((CHUNKS,)), dma((CHUNKS,)),
            dma((nsub,)), dma((nsub,)), dma((ny,)), dma((ny,)), dma((nz,)), dma((nz,)),
            dma((ny,)), dma((ny,)), dma((nsub,)), dma((nsub,)),
        ],
        compiler_params=pltpu.CompilerParams(
            collective_id=0, has_side_effects=True, vmem_limit_bytes=48 * 2**20
        ),
    )(operator, rhs, sizes, neighbours, kept)


BLOCK = 8


def three_parts(values):
    upper = values.astype(BF16)
    rest = values - upper.astype(F32)
    middle = rest.astype(BF16)
    lower = (rest - middle.astype(F32)).astype(BF16)
    return upper, middle, lower


def inverse_in_place(ref):
    n = ref.shape[0]
    b = BLOCK
    lane = lax.broadcasted_iota(jnp.int32, (b, n), 1)
    row = lax.broadcasted_iota(jnp.int32, (b, n), 0)
    wide_lane = lax.broadcasted_iota(jnp.int32, (n, n), 1)
    for start in range(0, n, b):
        panel = ref[start : start + b, :]
        columns = [jnp.broadcast_to(panel[:, start + j : start + j + 1], (b, n)) for j in range(b)]
        inside = (lane >= start) & (lane < start + b)
        work = jnp.where(inside, jnp.where(lane - start == row, 1.0, 0.0), panel)
        for j in range(b):
            inv = 1.0 / jnp.broadcast_to(columns[j][j : j + 1, :], (b, n))
            factor = columns[j] * inv
            here = row == j

            def eliminated(value):
                pivot = jnp.broadcast_to(value[j : j + 1, :], (b, n))
                return jnp.where(here, pivot * inv, value - factor * pivot)

            for k in range(j + 1, b):
                columns[k] = eliminated(columns[k])
            work = eliminated(work)
        column = jnp.where(inside, 0.0, jnp.where(lane < start, -panel, panel))
        ch, cm, cl = three_parts(column)
        wh, wm, wl = three_parts(work)
        lhs = jnp.concatenate([ch, ch, cm, cm, ch, cl], axis=0)
        rhs = jnp.concatenate([wh, wm, wh, wm, wl, wh], axis=0)
        update = dot(lhs, rhs, ((0,), (0,)))
        outside = (wide_lane < start) | (wide_lane >= start + b)
        ref[...] = jnp.where(outside, ref[...], 0.0) - update
        ref[start : start + b, :] = work


def solve_kernel(
    size_ref, sums_ref, keep_ref, rhs_ref, image_ref,
    solution_ref, residual_ref, direction_ref,
    inverse_ref, both_ref,
):
    nsub = sums_ref.shape[0]
    slab = sums_ref.shape[1] // 4
    n = inverse_ref.shape[0]
    keep = keep_ref[...].astype(F32)

    @pl.when(pl.program_id(0) == 0)
    def _():
        def matrix(k):
            return jnp.concatenate([sums_ref[s, k * slab : (k + 1) * slab, :] for s in range(nsub)], axis=0)

        curvature = matrix(0)
        rows = lax.broadcasted_iota(jnp.int32, (n, n), 0)
        lanes = lax.broadcasted_iota(jnp.int32, (n, n), 1)
        dropped = jnp.where(rows == lanes, 1.0 - keep, 0.0)
        inverse_ref[...] = 0.5 * (curvature + curvature.T) + dropped
        inverse_in_place(inverse_ref)
        inverse = inverse_ref[...]
        weights = dot(inverse, matrix(1), precision=HIGHEST)
        coupled = matrix(3) - dot(matrix(2), weights, precision=HIGHEST)
        both_ref[:, :n] = weights
        both_ref[:, n:] = dot(inverse, coupled, precision=HIGHEST)

    t, breadth = rhs_ref.shape[1:]
    rows = lax.broadcasted_iota(jnp.int32, (t, breadth), 0) + pl.program_id(0) * t
    live = jnp.where(rows < size_ref[0], rhs_ref[0], 0.0)
    rounded = (live * keep).astype(BF16).astype(F32)
    spread = dot(rounded, both_ref[...], precision=HIGHEST)
    residual = live - dot(image_ref[...], both_ref[:, :n], precision=HIGHEST)
    solution_ref[0] = spread[:, :n]
    residual_ref[0] = residual
    direction_ref[0] = residual - spread[:, n:]


def solve(sizes, sums, kept, rhs, image):
    _, height, breadth = rhs.shape
    tiles = 4
    tile = height // tiles
    whole = pl.BlockSpec((1, tile, breadth), lambda i: (0, i, 0))
    return pl.pallas_call(
        solve_kernel,
        name="solve_and_update",
        grid=(tiles,),
        out_shape=[jax.ShapeDtypeStruct(rhs.shape, F32)] * 3,
        in_specs=[
            pl.BlockSpec(memory_space=pltpu.SMEM),
            pl.BlockSpec(sums.shape, lambda i: (0, 0, 0)),
            pl.BlockSpec((1, breadth), lambda i: (0, 0)),
            whole,
            pl.BlockSpec((tile, breadth), lambda i: (i, 0)),
        ],
        out_specs=[whole] * 3,
        scratch_shapes=[pltpu.VMEM((breadth, breadth), F32), pltpu.VMEM((breadth, 2 * breadth), F32)],
    )(sizes, sums, kept, rhs, image)


def per_device(ny, nz, nx, nc, operator, rhs, interface_sizes, neighbour_rows, kept_columns):
    image, sums = communicate(operator, rhs, interface_sizes, neighbour_rows, kept_columns, ny, nz, nx, nc)
    return tuple(solve(interface_sizes, sums, kept_columns, rhs, image))


def solution(mesh, grid=(8, 12, 4, 2)):
    finer = Mesh(mesh.devices.reshape(grid), AXES)
    in_specs = (P(AXES, None, None), P(AXES, None, None), P(AXES), P(AXES, None), P())
    out_specs = (P(AXES, None, None),) * 3
    return jax.shard_map(
        functools.partial(per_device, *grid), mesh=finer, in_specs=in_specs, out_specs=out_specs, check_vma=False
    )
```

```python
import functools

import jax
import jax.numpy as jnp
from jax import lax
from jax.experimental import pallas as pl
from jax.experimental.pallas import tpu as pltpu
from jax.sharding import Mesh
from jax.sharding import PartitionSpec as P

AXES = ("y", "z", "x", "core")
F32 = jnp.float32
BF16 = jnp.bfloat16
HIGHEST = lax.Precision.HIGHEST
CHUNKS = 4
stiffness = 1.0


def dot(a, b, contract=((1,), (0,)), precision=None):
    return lax.dot_general(a, b, (contract, ((), ())), precision=precision, preferred_element_type=F32)


def three_parts(values):
    upper = values.astype(BF16)
    rest = values - upper.astype(F32)
    middle = rest.astype(BF16)
    lower = (rest - middle.astype(F32)).astype(BF16)
    return upper, middle, lower


def two_parts(values):
    upper = values.astype(BF16)
    return upper, (values - upper.astype(F32)).astype(BF16)


def sweep_block(k, ref):
    n = ref.shape[0]
    b = BLOCK
    start = pl.multiple_of(k * b, b)
    lane = lax.broadcasted_iota(jnp.int32, (b, n), 1)
    row = lax.broadcasted_iota(jnp.int32, (b, n), 0)
    wide_lane = lax.broadcasted_iota(jnp.int32, (n, n), 1)
    panel = ref[pl.ds(start, b), :]
    turned = pltpu.roll(panel, lax.rem(n - start, n), axis=1)
    columns = [jnp.broadcast_to(turned[:, j : j + 1], (b, n)) for j in range(b)]
    inside = (lane >= start) & (lane < start + b)
    work = jnp.where(inside, jnp.where(lane - start == row, 1.0, 0.0), panel)
    for j in range(b):
        inv = 1.0 / jnp.broadcast_to(columns[j][j : j + 1, :], (b, n))
        factor = columns[j] * inv
        here = row == j

        def eliminated(value):
            pivot = jnp.broadcast_to(value[j : j + 1, :], (b, n))
            return jnp.where(here, pivot * inv, value - factor * pivot)

        for i in range(j + 1, b):
            columns[i] = eliminated(columns[i])
        work = eliminated(work)
    column = jnp.where(inside, 0.0, jnp.where(lane < start, -panel, panel))
    ch, cm, cl = three_parts(column)
    wh, wm, wl = three_parts(work)
    lhs = jnp.concatenate([ch, ch, cm, cm, ch, cl], axis=0)
    rhs = jnp.concatenate([wh, wm, wh, wm, wl, wh], axis=0)
    update = dot(lhs, rhs, ((0,), (0,)))
    outside = (wide_lane < start) | (wide_lane >= start + b)
    ref[...] = jnp.where(outside, ref[...], 0.0) - update
    ref[pl.ds(start, b), :] = work


def comm_kernel(
    ny, nz, nx, nc,
    op_hbm, rhs_hbm, size_ref, nbr_hbm, keep_hbm,
    live_ref, image_ref, inverse_ref, rest_ref,
    op_ref, pt_ref, pm_ref, rounded_ref, ahead_ref, behind_ref, right_ref, nbr_ref, keep_ref,
    cgram_ref, cxin_ref, cy_ref, cyin_ref, cz_ref, czin_ref, csum_ref,
    gram_ref, xin_ref, ychunk_ref, yin_ref, zown_ref, zin_ref, part_ref,
    in_sem, f_send, f_recv, b_send, b_recv,
    cxs, cxr, cys, cyr, czs, czr, cxs2, cxr2,
    xs, xr, ys, yr, zs, zr, ys2, yr2, xs2, xr2,
):
    y, z, x, core = (lax.axis_index(a) for a in AXES)
    clu = y * nz + z
    nclu = ny * nz
    nsub = nx * nc
    sub = x * nc + core
    nxt = lax.rem(clu + 1, nclu)
    prv = lax.rem(clu + nclu - 1, nclu)

    def at_clu(c):
        return (c // nz, lax.rem(c, nz), x, core)

    def at_sub(s):
        return (y, z, s // nc, lax.rem(s, nc))

    next_id, prev_id = at_clu(nxt), at_clu(prv)
    sub_ids = [None] + [at_sub(lax.rem(sub + d, nsub)) for d in range(1, nsub)]
    y_ids = [None] + [(lax.rem(y + d, ny), z, x, core) for d in range(1, ny)]
    z_ids = [None] + [(y, lax.rem(z + d, nz), x, core) for d in range(1, nz)]

    barrier = pltpu.get_barrier_semaphore()
    greeted = [next_id, prev_id] + sub_ids[1:] + y_ids[1:] + z_ids[1:]
    for device in greeted:
        pl.semaphore_signal(barrier, inc=1, device_id=device, device_id_type=pl.DeviceIdType.MESH)

    loads = [
        pltpu.make_async_copy(src, dst, in_sem.at[i])
        for i, (src, dst) in enumerate(
            [(rhs_hbm.at[0], live_ref), (keep_hbm, keep_ref), (nbr_hbm, nbr_ref), (op_hbm.at[0], op_ref)]
        )
    ]
    for load in loads:
        load.start()

    height, breadth = rounded_ref.shape
    step = height // CHUNKS
    size = size_ref[0]
    tiles = [pl.ds(t * step, step) for t in range(CHUNKS)]

    def remote(src, dst, send, recv, device):
        return pltpu.make_async_remote_copy(
            src_ref=src, dst_ref=dst, send_sem=send, recv_sem=recv,
            device_id=device, device_id_type=pl.DeviceIdType.MESH,
        )

    for load in loads[:3]:
        load.wait()
    keep = keep_ref[...].astype(F32)
    for t, rows in enumerate(tiles):
        index = lax.broadcasted_iota(jnp.int32, (step, breadth), 0) + t * step
        live = jnp.where(index < size, live_ref[rows, :], 0.0)
        live_ref[rows, :] = live
        rounded_ref[rows, :] = (live * keep).astype(BF16)
        index = lax.broadcasted_iota(jnp.int32, (step, height), 0) + t * step
        pt_ref[rows, :] = jnp.where(index == nbr_ref[...], 1.0, 0.0).astype(BF16)
    for rows in tiles:
        ahead_ref[rows, :] = dot(pt_ref[rows, :], rounded_ref[...]).astype(BF16)

    pl.semaphore_wait(barrier, len(greeted))

    forward, backward = [], []
    for t, rows in enumerate(tiles):
        forward.append(remote(rounded_ref.at[rows, :], behind_ref.at[rows, :], f_send.at[t], f_recv.at[t], next_id))
        backward.append(remote(ahead_ref.at[rows, :], right_ref.at[rows, :], b_send.at[t], b_recv.at[t], prev_id))
        forward[t].start()
        backward[t].start()

    tall = jnp.broadcast_to(nbr_ref[...].astype(F32), (breadth, height)).T
    for c in range(0, height, breadth):
        lanes = (lax.broadcasted_iota(jnp.int32, (height, breadth), 1) + c).astype(F32)
        pm_ref[:, c : c + breadth] = jnp.where(tall == lanes, 1.0, 0.0).astype(BF16)
    has_prev = clu > 0
    has_next = clu < nclu - 1
    degree = has_prev.astype(F32) + has_next.astype(F32)
    loads[3].wait()
    for rows in tiles:
        product = dot(op_ref[rows, :], rounded_ref[...])
        image_ref[rows, :] = product + stiffness * degree * rounded_ref[rows, :].astype(F32)

    prev_scale = jnp.where(has_prev, stiffness, 0.0).astype(F32)
    next_scale = jnp.where(has_next, stiffness, 0.0).astype(F32)
    for t, rows in enumerate(tiles):
        backward[t].wait_recv()
        image_ref[rows, :] = image_ref[rows, :] - next_scale * right_ref[rows, :].astype(F32)
        forward[t].wait_recv()
        if t < CHUNKS - 1:
            block = behind_ref[rows, :]
            for out in tiles:
                left = dot(pm_ref[out, rows], block)
                image_ref[out, :] = image_ref[out, :] - prev_scale * left
    block = behind_ref[tiles[-1], :]
    gram = None
    for t, out in enumerate(tiles):
        left = dot(pm_ref[out, tiles[-1]], block)
        index = lax.broadcasted_iota(jnp.int32, (step, breadth), 0) + t * step
        image = jnp.where(index < size, image_ref[out, :] - prev_scale * left, 0.0)
        image_ref[out, :] = image
        lhs = jnp.concatenate([rounded_ref[out, :].astype(F32), image], axis=1)
        rhs = jnp.concatenate([image, live_ref[out, :]], axis=1)
        term = dot(lhs, rhs, ((0,), (0,)), HIGHEST)
        gram = term if gram is None else gram + term
    curvature = gram[:breadth, :breadth]
    others = (gram[:breadth, breadth:], gram[breadth:, :breadth], gram[breadth:, breadth:])
    slab = breadth // nsub
    for s in range(nsub):
        cgram_ref[s] = curvature[s * slab : (s + 1) * slab, :]

    sent = forward + backward

    def scatter(source, place, count, landing, send, recv, ids):
        copies = []
        for d in range(1, count):
            peer = lax.rem(place + d, count)
            copies.append(remote(source.at[peer], landing.at[d], send.at[d], recv.at[d], ids[d]))
            copies[-1].start()
        sent.extend(copies)
        return copies

    def spread(source, count, landing, send, recv, ids):
        copies = []
        for d in range(1, count):
            copies.append(remote(source, landing.at[d], send.at[d], recv.at[d], ids[d]))
            copies[-1].start()
        sent.extend(copies)
        return copies

    def share(array, place, count, send, recv, ids):
        copies = []
        for d in range(1, count):
            copies.append(remote(array.at[place], array.at[place], send.at[d], recv.at[d], ids[d]))
            copies[-1].start()
        sent.extend(copies)
        return copies

    def add_up(total, copies, landing):
        for d, copy in enumerate(copies, 1):
            copy.wait_recv()
            total = total + landing[d]
        return total

    cx = scatter(cgram_ref, sub, nsub, cxin_ref, cxs, cxr, sub_ids)
    for s in range(nsub):
        for k, piece in enumerate(others):
            gram_ref[s, k * slab : (k + 1) * slab, :] = piece[s * slab : (s + 1) * slab, :]
    rx = scatter(gram_ref, sub, nsub, xin_ref, xs, xr, sub_ids)

    cy_ref[...] = add_up(cgram_ref[sub], cx, cxin_ref)
    cy = spread(cy_ref, ny, cyin_ref, cys, cyr, y_ids)
    total = add_up(gram_ref[sub], rx, xin_ref)
    rows_y = total.shape[0] // ny
    for v in range(ny):
        ychunk_ref[v] = total[v * rows_y : (v + 1) * rows_y, :]
    ry = scatter(ychunk_ref, y, ny, yin_ref, ys, yr, y_ids)

    cz_ref[...] = add_up(cy_ref[...], cy, cyin_ref)
    cz = spread(cz_ref, nz, czin_ref, czs, czr, z_ids)
    zown_ref[...] = add_up(ychunk_ref[y], ry, yin_ref)
    rz = spread(zown_ref, nz, zin_ref, zs, zr, z_ids)

    csum_ref[sub] = add_up(cz_ref[...], cz, czin_ref)
    cx2 = share(csum_ref, sub, nsub, cxs2, cxr2, sub_ids)
    part_ref[y] = add_up(zown_ref[...], rz, zin_ref)
    ry2 = share(part_ref, y, ny, ys2, yr2, y_ids)

    for copy in cx2:
        copy.wait_recv()
    summed = jnp.concatenate([csum_ref[s] for s in range(nsub)], axis=0)
    rows = lax.broadcasted_iota(jnp.int32, (breadth, breadth), 0)
    lanes = lax.broadcasted_iota(jnp.int32, (breadth, breadth), 1)
    inverse_ref[...] = 0.5 * (summed + summed.T) + jnp.where(rows == lanes, 1.0 - keep, 0.0)

    def sweep(first, last):
        def one(k, carry):
            sweep_block(k, inverse_ref)
            return carry

        lax.fori_loop(first, last, one, 0)

    blocks = breadth // BLOCK
    sweep(0, blocks // 4)
    for copy in ry2:
        copy.wait_recv()
    for v in range(ny):
        rest_ref[sub, v * rows_y : (v + 1) * rows_y, :] = part_ref[v]
    rx2 = share(rest_ref, sub, nsub, xs2, xr2, sub_ids)
    sweep(blocks // 4, blocks)
    for copy in rx2:
        copy.wait_recv()
    for copy in sent:
        copy.wait_send()


def communicate(operator, rhs, sizes, neighbours, kept, ny, nz, nx, nc):
    height, breadth = rhs.shape[1:]
    nsub = nx * nc
    slab = breadth // nsub
    piece = 3 * slab // ny
    vmem = pl.BlockSpec(memory_space=pltpu.VMEM)
    hbm = pl.BlockSpec(memory_space=pltpu.HBM)
    dma = pltpu.SemaphoreType.DMA
    tall = (height, breadth)
    return pl.pallas_call(
        functools.partial(comm_kernel, ny, nz, nx, nc),
        name="exchange_and_sums",
        out_shape=(
            jax.ShapeDtypeStruct(tall, F32),
            jax.ShapeDtypeStruct(tall, F32),
            jax.ShapeDtypeStruct((breadth, breadth), F32),
            jax.ShapeDtypeStruct((nsub, 3 * slab, breadth), F32),
        ),
        in_specs=[hbm, hbm, pl.BlockSpec(memory_space=pltpu.SMEM), hbm, hbm],
        out_specs=(vmem,) * 4,
        scratch_shapes=[
            pltpu.VMEM((height, height), BF16),
            pltpu.VMEM((height, height), BF16),
            pltpu.VMEM((height, height), BF16),
            pltpu.VMEM(tall, BF16),
            pltpu.VMEM(tall, BF16),
            pltpu.VMEM(tall, BF16),
            pltpu.VMEM(tall, BF16),
            pltpu.VMEM((1, height), jnp.int32),
            pltpu.VMEM((1, breadth), jnp.int32),
            pltpu.VMEM((nsub, slab, breadth), F32),
            pltpu.VMEM((nsub, slab, breadth), F32),
            pltpu.VMEM((slab, breadth), F32),
            pltpu.VMEM((ny, slab, breadth), F32),
            pltpu.VMEM((slab, breadth), F32),
            pltpu.VMEM((nz, slab, breadth), F32),
            pltpu.VMEM((nsub, slab, breadth), F32),
            pltpu.VMEM((nsub, 3 * slab, breadth), F32),
            pltpu.VMEM((nsub, 3 * slab, breadth), F32),
            pltpu.VMEM((ny, piece, breadth), F32),
            pltpu.VMEM((ny, piece, breadth), F32),
            pltpu.VMEM((piece, breadth), F32),
            pltpu.VMEM((nz, piece, breadth), F32),
            pltpu.VMEM((ny, piece, breadth), F32),
            dma((4,)),
            dma((CHUNKS,)), dma((CHUNKS,)), dma((CHUNKS,)), dma((CHUNKS,)),
            dma((nsub,)), dma((nsub,)), dma((ny,)), dma((ny,)), dma((nz,)), dma((nz,)), dma((nsub,)), dma((nsub,)),
            dma((nsub,)), dma((nsub,)), dma((ny,)), dma((ny,)), dma((nz,)), dma((nz,)),
            dma((ny,)), dma((ny,)), dma((nsub,)), dma((nsub,)),
        ],
        compiler_params=pltpu.CompilerParams(
            collective_id=0, has_side_effects=True, vmem_limit_bytes=55230000
        ),
    )(operator, rhs, sizes, neighbours, kept)


BLOCK = 8


def update_kernel(
    live_ref, image_ref, inverse_ref, rest_ref, keep_ref,
    solution_hbm, residual_hbm, direction_hbm,
    solution_ref, residual_ref, direction_ref, sems,
):
    nsub, rows3 = rest_ref.shape[:2]
    slab = rows3 // 3
    keep = keep_ref[...].astype(F32)
    height = live_ref.shape[0]
    step = height // CHUNKS

    def matrix(k):
        return jnp.concatenate([rest_ref[s, k * slab : (k + 1) * slab, :] for s in range(nsub)], axis=0)

    inverse = inverse_ref[...]
    weights = dot(inverse, matrix(0), precision=HIGHEST)
    coupled = matrix(2) - dot(matrix(1), weights, precision=HIGHEST)
    correction = dot(inverse, coupled, precision=HIGHEST)
    wh, wm, wl = three_parts(weights)
    zh, zm, zl = three_parts(correction)
    n = weights.shape[0]
    wide = jnp.concatenate([wh, wm, wl, zh, zm, zl], axis=1)
    copies = []
    for t in range(CHUNKS):
        rows = pl.ds(t * step, step)
        live = live_ref[rows, :]
        rounded = (live * keep).astype(BF16)
        spread = dot(rounded, wide)
        ih, im, il = three_parts(image_ref[rows, :])
        first = dot(ih, wide[:, : 3 * n])
        second = dot(im, wide[:, : 2 * n])
        third = dot(il, wh)
        moved = first[:, :n] + (first[:, n : 2 * n] + second[:, :n]) + (first[:, 2 * n :] + second[:, n:] + third)
        residual = live - moved
        solution_ref[rows, :] = spread[:, :n] + spread[:, n : 2 * n] + spread[:, 2 * n : 3 * n]
        residual_ref[rows, :] = residual
        direction_ref[rows, :] = residual - (
            spread[:, 3 * n : 4 * n] + spread[:, 4 * n : 5 * n] + spread[:, 5 * n :]
        )
        for k, (src, dst) in enumerate(
            [(solution_ref, solution_hbm), (residual_ref, residual_hbm), (direction_ref, direction_hbm)]
        ):
            copies.append(pltpu.make_async_copy(src.at[rows, :], dst.at[0, rows, :], sems.at[k, t]))
            copies[-1].start()
    for copy in copies:
        copy.wait()


def update(live, image, inverse, rest, kept):
    vmem = pl.BlockSpec(memory_space=pltpu.VMEM)
    return pl.pallas_call(
        update_kernel,
        name="update",
        out_shape=[jax.ShapeDtypeStruct((1, *live.shape), F32)] * 3,
        in_specs=[vmem] * 5,
        out_specs=[pl.BlockSpec(memory_space=pltpu.HBM)] * 3,
        scratch_shapes=[pltpu.VMEM(live.shape, F32)] * 3 + [pltpu.SemaphoreType.DMA((3, CHUNKS))],
        compiler_params=pltpu.CompilerParams(vmem_limit_bytes=40 * 2**20),
    )(live, image, inverse, rest, kept)


def per_device(ny, nz, nx, nc, operator, rhs, interface_sizes, neighbour_rows, kept_columns):
    results = communicate(operator, rhs, interface_sizes, neighbour_rows, kept_columns, ny, nz, nx, nc)
    return tuple(update(*results, kept_columns))


def solution(mesh, grid=(8, 12, 4, 2)):
    finer = Mesh(mesh.devices.reshape(grid), AXES)
    in_specs = (P(AXES, None, None), P(AXES, None, None), P(AXES), P(AXES, None), P())
    out_specs = (P(AXES, None, None),) * 3
    return jax.shard_map(
        functools.partial(per_device, *grid), mesh=finer, in_specs=in_specs, out_specs=out_specs, check_vma=False
    )
```

```python
import functools

import jax
import jax.numpy as jnp
from jax import lax
from jax.experimental import pallas as pl
from jax.experimental.pallas import tpu as pltpu
from jax.sharding import Mesh
from jax.sharding import PartitionSpec as P

AXES = ("y", "z", "x", "core")
F32 = jnp.float32
BF16 = jnp.bfloat16
HIGHEST = lax.Precision.HIGHEST
CHUNKS = 4
stiffness = 1.0


def dot(a, b, contract=((1,), (0,)), precision=None):
    return lax.dot_general(a, b, (contract, ((), ())), precision=precision, preferred_element_type=F32)


def three_parts(values):
    upper = values.astype(BF16)
    rest = values - upper.astype(F32)
    middle = rest.astype(BF16)
    lower = (rest - middle.astype(F32)).astype(BF16)
    return upper, middle, lower


def two_parts(values):
    upper = values.astype(BF16)
    return upper, (values - upper.astype(F32)).astype(BF16)


def sweep_block(k, ref):
    n = ref.shape[0]
    b = BLOCK
    start = pl.multiple_of(k * b, b)
    lane = lax.broadcasted_iota(jnp.int32, (b, n), 1)
    row = lax.broadcasted_iota(jnp.int32, (b, n), 0)
    wide_lane = lax.broadcasted_iota(jnp.int32, (n, n), 1)
    panel = ref[pl.ds(start, b), :]
    turned = pltpu.roll(panel, lax.rem(n - start, n), axis=1)
    columns = [jnp.broadcast_to(turned[:, j : j + 1], (b, n)) for j in range(b)]
    inside = (lane >= start) & (lane < start + b)
    work = jnp.where(inside, jnp.where(lane - start == row, 1.0, 0.0), panel)
    for j in range(b):
        inv = 1.0 / jnp.broadcast_to(columns[j][j : j + 1, :], (b, n))
        factor = columns[j] * inv
        here = row == j

        def eliminated(value):
            pivot = jnp.broadcast_to(value[j : j + 1, :], (b, n))
            return jnp.where(here, pivot * inv, value - factor * pivot)

        for i in range(j + 1, b):
            columns[i] = eliminated(columns[i])
        work = eliminated(work)
    column = jnp.where(inside, 0.0, jnp.where(lane < start, -panel, panel))
    ch, cm, cl = three_parts(column)
    wh, wm, wl = three_parts(work)
    lhs = jnp.concatenate([ch, ch, cm, cm, ch, cl], axis=0)
    rhs = jnp.concatenate([wh, wm, wh, wm, wl, wh], axis=0)
    update = dot(lhs, rhs, ((0,), (0,)))
    outside = (wide_lane < start) | (wide_lane >= start + b)
    ref[...] = jnp.where(outside, ref[...], 0.0) - update
    ref[pl.ds(start, b), :] = work


def pack(matrix, ref):
    n = matrix.shape[0]
    half, count = n // 2, ref.shape[0]
    each = half // count
    matrix = 0.5 * (matrix + matrix.T)
    row = lax.broadcasted_iota(jnp.int32, (half, n), 0)
    lane = lax.broadcasted_iota(jnp.int32, (half, n), 1)
    upper = matrix[:half, :]
    turned = pltpu.roll(matrix[half:, :], half, axis=1)
    packed = jnp.where((lane < half) & (lane > row), turned, upper)
    diagonal = jnp.sum(jnp.where(lane == row, turned, 0.0), axis=0, keepdims=True)
    for s in range(count):
        ref[s, :each, :] = packed[s * each : (s + 1) * each, :]
        ref[s, each : each + 1, :] = diagonal


def unpack(ref):
    count, each, n = ref.shape
    each, half = each - 1, n // 2
    packed = jnp.concatenate([ref[s, :each, :] for s in range(count)], axis=0)
    diagonal = ref[0, each : each + 1, :]
    row = lax.broadcasted_iota(jnp.int32, (half, n), 0)
    lane = lax.broadcasted_iota(jnp.int32, (half, n), 1)
    turned = jnp.concatenate([packed, packed], axis=0).T
    upper = jnp.where((lane < half) & (lane > row), turned[:half, :], packed)
    lower = jnp.where(lane > row, packed, jnp.where(lane == row, diagonal, turned[:half, :]))
    lower = jnp.where(lane < half, turned[half:, :], pltpu.roll(lower, half, axis=1))
    return jnp.concatenate([upper, lower], axis=0)


def comm_kernel(
    ny, nz, nx, nc,
    op_hbm, rhs_hbm, size_ref, nbr_hbm, keep_hbm,
    live_ref, rounded_ref, image_ref, inverse_ref, rest_ref,
    op_ref, pt_ref, pm_ref, ahead_ref, behind_ref, right_ref, nbr_ref, keep_ref,
    cgram_ref, cxin_ref, cy_ref, cyin_ref, cz_ref, czin_ref, csum_ref,
    gram_ref, xin_ref, ychunk_ref, yin_ref, zown_ref, zin_ref, part_ref,
    y_known, z_known, in_sem, f_send, f_recv, b_send, b_recv,
    cxs, cxr, cys, cyr, czs, czr, cxs2, cxr2,
    xs, xr, ys, yr, zs, zr, ys2, yr2, xs2, xr2,
):
    y, z, x, core = (lax.axis_index(a) for a in AXES)
    clu = y * nz + z
    nclu = ny * nz
    nsub = nx * nc
    sub = x * nc + core
    nxt = lax.rem(clu + 1, nclu)
    prv = lax.rem(clu + nclu - 1, nclu)

    def at_clu(c):
        return (c // nz, lax.rem(c, nz), x, core)

    def at_sub(s):
        return (y, z, s // nc, lax.rem(s, nc))

    next_id, prev_id = at_clu(nxt), at_clu(prv)
    sub_ids = [None] + [at_sub(lax.rem(sub + d, nsub)) for d in range(1, nsub)]
    y_ids = [None] + [(lax.rem(y + d, ny), z, x, core) for d in range(1, ny)]
    z_ids = [None] + [(y, lax.rem(z + d, nz), x, core) for d in range(1, nz)]

    barrier = pltpu.get_barrier_semaphore()
    greeted = [next_id, prev_id, y_ids[1], y_ids[-1], z_ids[1], z_ids[-1]] + sub_ids[1:]

    def signal(semaphore, device):
        pl.semaphore_signal(semaphore, inc=1, device_id=device, device_id_type=pl.DeviceIdType.MESH)

    for device in greeted:
        signal(barrier, device)

    loads = [
        pltpu.make_async_copy(src, dst, in_sem.at[i])
        for i, (src, dst) in enumerate(
            [(rhs_hbm.at[0], live_ref), (keep_hbm, keep_ref), (nbr_hbm, nbr_ref), (op_hbm.at[0], op_ref)]
        )
    ]
    for load in loads:
        load.start()

    height, breadth = rounded_ref.shape
    step = height // CHUNKS
    size = size_ref[0]
    tiles = [pl.ds(t * step, step) for t in range(CHUNKS)]

    def remote(src, dst, send, recv, device):
        return pltpu.make_async_remote_copy(
            src_ref=src, dst_ref=dst, send_sem=send, recv_sem=recv,
            device_id=device, device_id_type=pl.DeviceIdType.MESH,
        )

    for load in loads[:3]:
        load.wait()
    keep = keep_ref[...].astype(F32)
    for t, rows in enumerate(tiles):
        index = lax.broadcasted_iota(jnp.int32, (step, breadth), 0) + t * step
        live = jnp.where(index < size, live_ref[rows, :], 0.0)
        live_ref[rows, :] = live
        rounded_ref[rows, :] = (live * keep).astype(BF16)
        index = lax.broadcasted_iota(jnp.int32, (step, height), 0) + t * step
        pt_ref[rows, :] = jnp.where(index == nbr_ref[...], 1.0, 0.0).astype(BF16)
    for rows in tiles:
        ahead_ref[rows, :] = dot(pt_ref[rows, :], rounded_ref[...]).astype(BF16)

    pl.semaphore_wait(barrier, len(greeted))

    forward, backward = [], []
    for t, rows in enumerate(tiles):
        forward.append(remote(rounded_ref.at[rows, :], behind_ref.at[rows, :], f_send.at[t], f_recv.at[t], next_id))
        backward.append(remote(ahead_ref.at[rows, :], right_ref.at[rows, :], b_send.at[t], b_recv.at[t], prev_id))
        forward[t].start()
        backward[t].start()

    tall = jnp.broadcast_to(nbr_ref[...].astype(F32), (breadth, height)).T
    for c in range(0, height, breadth):
        lanes = (lax.broadcasted_iota(jnp.int32, (height, breadth), 1) + c).astype(F32)
        pm_ref[:, c : c + breadth] = jnp.where(tall == lanes, 1.0, 0.0).astype(BF16)
    has_prev = clu > 0
    has_next = clu < nclu - 1
    degree = has_prev.astype(F32) + has_next.astype(F32)
    loads[3].wait()
    for rows in tiles:
        product = dot(op_ref[rows, :], rounded_ref[...])
        image_ref[rows, :] = product + stiffness * degree * rounded_ref[rows, :].astype(F32)

    for r in range(max(ny, nz) // 2 - 1):
        rings = [(known, ids) for known, ids, n in ((y_known, y_ids, ny), (z_known, z_ids, nz)) if r < n // 2 - 1]
        for known, ids in rings:
            signal(known.at[2 * r], ids[1])
            signal(known.at[2 * r + 1], ids[-1])
        for known, ids in rings:
            pl.semaphore_wait(known.at[2 * r], 1)
            pl.semaphore_wait(known.at[2 * r + 1], 1)

    prev_scale = jnp.where(has_prev, stiffness, 0.0).astype(F32)
    next_scale = jnp.where(has_next, stiffness, 0.0).astype(F32)
    for t, rows in enumerate(tiles):
        backward[t].wait_recv()
        image_ref[rows, :] = image_ref[rows, :] - next_scale * right_ref[rows, :].astype(F32)
        forward[t].wait_recv()
        if t < CHUNKS - 1:
            block = behind_ref[rows, :]
            for out in tiles:
                left = dot(pm_ref[out, rows], block)
                image_ref[out, :] = image_ref[out, :] - prev_scale * left
    block = behind_ref[tiles[-1], :]
    curvature = None
    for t, out in enumerate(tiles):
        left = dot(pm_ref[out, tiles[-1]], block)
        index = lax.broadcasted_iota(jnp.int32, (step, breadth), 0) + t * step
        image = jnp.where(index < size, image_ref[out, :] - prev_scale * left, 0.0)
        image_ref[out, :] = image
        term = dot(rounded_ref[out, :], jnp.concatenate(two_parts(image), axis=1), ((0,), (0,)))
        curvature = term if curvature is None else curvature + term
    curvature = curvature[:, :breadth] + curvature[:, breadth:]
    slab = breadth // nsub
    half = breadth // 2
    pack(curvature, cgram_ref)

    sent = forward + backward

    def scatter(source, place, count, landing, send, recv, ids):
        copies = []
        for d in range(1, count):
            peer = lax.rem(place + d, count)
            copies.append(remote(source.at[peer], landing.at[d], send.at[d], recv.at[d], ids[d]))
            copies[-1].start()
        sent.extend(copies)
        return copies

    def spread(source, count, landing, send, recv, ids):
        copies = []
        for d in range(1, count):
            copies.append(remote(source, landing.at[d], send.at[d], recv.at[d], ids[d]))
            copies[-1].start()
        sent.extend(copies)
        return copies

    def share(array, place, count, send, recv, ids):
        copies = []
        for d in range(1, count):
            copies.append(remote(array.at[place], array.at[place], send.at[d], recv.at[d], ids[d]))
            copies[-1].start()
        sent.extend(copies)
        return copies

    def add_up(total, copies, landing):
        for d, copy in enumerate(copies, 1):
            copy.wait_recv()
            total = total + landing[d]
        return total

    cx = scatter(cgram_ref, sub, nsub, cxin_ref, cxs, cxr, sub_ids)
    gram = None
    for out in tiles:
        ih, im = two_parts(image_ref[out, :])
        lh, lm = two_parts(live_ref[out, :])
        lhs = jnp.concatenate([rounded_ref[out, :], ih, im], axis=1)
        rhs = jnp.concatenate([lh, ih, lm, im], axis=1)
        term = dot(lhs, rhs, ((0,), (0,)))
        gram = term if gram is None else gram + term
    first = gram[: 2 * breadth, : 2 * breadth] + gram[: 2 * breadth, 2 * breadth :]
    second = first[breadth:, :] + gram[2 * breadth :, : 2 * breadth]
    others = (first[:breadth, :breadth], second[:, breadth:], second[:, :breadth])
    for s in range(nsub):
        for k, piece in enumerate(others):
            gram_ref[s, k * slab : (k + 1) * slab, :] = piece[s * slab : (s + 1) * slab, :]
    rx = scatter(gram_ref, sub, nsub, xin_ref, xs, xr, sub_ids)

    cy_ref[...] = add_up(cgram_ref[sub], cx, cxin_ref)
    cy = spread(cy_ref, ny, cyin_ref, cys, cyr, y_ids)
    total = add_up(gram_ref[sub], rx, xin_ref)
    rows_y = total.shape[0] // ny
    for v in range(ny):
        ychunk_ref[v] = total[v * rows_y : (v + 1) * rows_y, :]
    ry = scatter(ychunk_ref, y, ny, yin_ref, ys, yr, y_ids)

    cz_ref[...] = add_up(cy_ref[...], cy, cyin_ref)
    cz = spread(cz_ref, nz, czin_ref, czs, czr, z_ids)
    zown_ref[...] = add_up(ychunk_ref[y], ry, yin_ref)
    rz = spread(zown_ref, nz, zin_ref, zs, zr, z_ids)

    csum_ref[sub] = add_up(cz_ref[...], cz, czin_ref)
    cx2 = share(csum_ref, sub, nsub, cxs2, cxr2, sub_ids)
    part_ref[y] = add_up(zown_ref[...], rz, zin_ref)
    ry2 = share(part_ref, y, ny, ys2, yr2, y_ids)

    for copy in cx2:
        copy.wait_recv()
    summed = unpack(csum_ref)
    rows = lax.broadcasted_iota(jnp.int32, (breadth, breadth), 0)
    lanes = lax.broadcasted_iota(jnp.int32, (breadth, breadth), 1)
    inverse_ref[...] = summed + jnp.where(rows == lanes, 1.0 - keep, 0.0)

    def sweep(first, last):
        def one(k, carry):
            sweep_block(k, inverse_ref)
            return carry

        lax.fori_loop(first, last, one, 0)

    blocks = breadth // BLOCK
    sweep(0, blocks // 4)
    for copy in ry2:
        copy.wait_recv()
    for v in range(ny):
        rest_ref[sub, v * rows_y : (v + 1) * rows_y, :] = part_ref[v]
    rx2 = share(rest_ref, sub, nsub, xs2, xr2, sub_ids)
    sweep(blocks // 4, blocks)
    for copy in rx2:
        copy.wait_recv()
    for copy in sent:
        copy.wait_send()


def hbm_only(array):
    return pltpu.with_memory_space_constraint(array, pltpu.HBM)


def communicate(operator, rhs, sizes, neighbours, kept, ny, nz, nx, nc):
    height, breadth = rhs.shape[1:]
    nsub = nx * nc
    slab = breadth // nsub
    piece = 3 * slab // ny
    packed = slab // 2 + 1
    signals = pltpu.SemaphoreType.REGULAR
    vmem = pl.BlockSpec(memory_space=pltpu.VMEM)
    hbm = pl.BlockSpec(memory_space=pltpu.HBM)
    dma = pltpu.SemaphoreType.DMA
    tall = (height, breadth)
    return pl.pallas_call(
        functools.partial(comm_kernel, ny, nz, nx, nc),
        name="exchange_and_sums",
        out_shape=(
            jax.ShapeDtypeStruct(tall, F32),
            jax.ShapeDtypeStruct(tall, BF16),
            jax.ShapeDtypeStruct(tall, F32),
            jax.ShapeDtypeStruct((breadth, breadth), F32),
            jax.ShapeDtypeStruct((nsub, 3 * slab, breadth), F32),
        ),
        in_specs=[hbm, hbm, pl.BlockSpec(memory_space=pltpu.SMEM), hbm, hbm],
        out_specs=(vmem,) * 5,
        scratch_shapes=[
            pltpu.VMEM((height, height), BF16),
            pltpu.VMEM((height, height), BF16),
            pltpu.VMEM((height, height), BF16),
            pltpu.VMEM(tall, BF16),
            pltpu.VMEM(tall, BF16),
            pltpu.VMEM(tall, BF16),
            pltpu.VMEM((1, height), jnp.int32),
            pltpu.VMEM((1, breadth), jnp.int32),
            pltpu.VMEM((nsub, packed, breadth), F32),
            pltpu.VMEM((nsub, packed, breadth), F32),
            pltpu.VMEM((packed, breadth), F32),
            pltpu.VMEM((ny, packed, breadth), F32),
            pltpu.VMEM((packed, breadth), F32),
            pltpu.VMEM((nz, packed, breadth), F32),
            pltpu.VMEM((nsub, packed, breadth), F32),
            pltpu.VMEM((nsub, 3 * slab, breadth), F32),
            pltpu.VMEM((nsub, 3 * slab, breadth), F32),
            pltpu.VMEM((ny, piece, breadth), F32),
            pltpu.VMEM((ny, piece, breadth), F32),
            pltpu.VMEM((piece, breadth), F32),
            pltpu.VMEM((nz, piece, breadth), F32),
            pltpu.VMEM((ny, piece, breadth), F32),
            signals((max(ny - 2, 2),)), signals((max(nz - 2, 2),)),
            dma((4,)),
            dma((CHUNKS,)), dma((CHUNKS,)), dma((CHUNKS,)), dma((CHUNKS,)),
            dma((nsub,)), dma((nsub,)), dma((ny,)), dma((ny,)), dma((nz,)), dma((nz,)), dma((nsub,)), dma((nsub,)),
            dma((nsub,)), dma((nsub,)), dma((ny,)), dma((ny,)), dma((nz,)), dma((nz,)),
            dma((ny,)), dma((ny,)), dma((nsub,)), dma((nsub,)),
        ],
        compiler_params=pltpu.CompilerParams(
            collective_id=0, has_side_effects=True, vmem_limit_bytes=40 * 2**20
        ),
    )(hbm_only(operator), hbm_only(rhs), sizes, hbm_only(neighbours), hbm_only(kept))


BLOCK = 16


def update_kernel(
    live_ref, rounded_ref, image_ref, inverse_ref, rest_ref,
    solution_hbm, residual_hbm, direction_hbm,
    solution_ref, residual_ref, direction_ref, sems,
):
    nsub, rows3 = rest_ref.shape[:2]
    slab = rows3 // 3
    height = live_ref.shape[0]
    step = height // CHUNKS

    def matrix(k):
        return jnp.concatenate([rest_ref[s, k * slab : (k + 1) * slab, :] for s in range(nsub)], axis=0)

    inverse = inverse_ref[...]
    weights = dot(inverse, matrix(0), precision=HIGHEST)
    coupled = matrix(2) - dot(matrix(1), weights, precision=HIGHEST)
    correction = dot(inverse, coupled, precision=HIGHEST)
    wh, wm, wl = three_parts(weights)
    zh, zm, zl = three_parts(correction)
    n = weights.shape[0]
    wide = jnp.concatenate([wh, wm, wl, zh, zm, zl], axis=1)
    copies = []
    for t in range(CHUNKS):
        rows = pl.ds(t * step, step)
        live = live_ref[rows, :]
        spread = dot(rounded_ref[rows, :], wide)
        ih, im, il = three_parts(image_ref[rows, :])
        first = dot(ih, wide[:, : 3 * n])
        second = dot(im, wide[:, : 2 * n])
        third = dot(il, wh)
        moved = first[:, :n] + (first[:, n : 2 * n] + second[:, :n]) + (first[:, 2 * n :] + second[:, n:] + third)
        residual = live - moved
        solution_ref[rows, :] = spread[:, :n] + spread[:, n : 2 * n] + spread[:, 2 * n : 3 * n]
        residual_ref[rows, :] = residual
        direction_ref[rows, :] = residual - (
            spread[:, 3 * n : 4 * n] + spread[:, 4 * n : 5 * n] + spread[:, 5 * n :]
        )
        for k, (src, dst) in enumerate(
            [(solution_ref, solution_hbm), (residual_ref, residual_hbm), (direction_ref, direction_hbm)]
        ):
            copies.append(pltpu.make_async_copy(src.at[rows, :], dst.at[0, rows, :], sems.at[k, t]))
            copies[-1].start()
    for copy in copies:
        copy.wait()


def update(live, rounded, image, inverse, rest):
    vmem = pl.BlockSpec(memory_space=pltpu.VMEM)
    return pl.pallas_call(
        update_kernel,
        name="update",
        out_shape=[jax.ShapeDtypeStruct((1, *live.shape), F32)] * 3,
        in_specs=[vmem] * 5,
        out_specs=[pl.BlockSpec(memory_space=pltpu.HBM)] * 3,
        scratch_shapes=[pltpu.VMEM(live.shape, F32)] * 3 + [pltpu.SemaphoreType.DMA((3, CHUNKS))],
        compiler_params=pltpu.CompilerParams(vmem_limit_bytes=40 * 2**20),
    )(live, rounded, image, inverse, rest)


def per_device(ny, nz, nx, nc, operator, rhs, interface_sizes, neighbour_rows, kept_columns):
    results = communicate(operator, rhs, interface_sizes, neighbour_rows, kept_columns, ny, nz, nx, nc)
    return tuple(update(*results))


def solution(mesh, grid=(8, 12, 4, 2)):
    finer = Mesh(mesh.devices.reshape(grid), AXES)
    in_specs = (P(AXES, None, None), P(AXES, None, None), P(AXES), P(AXES, None), P())
    out_specs = (P(AXES, None, None),) * 3
    return jax.shard_map(
        functools.partial(per_device, *grid), mesh=finer, in_specs=in_specs, out_specs=out_specs, check_vma=False
    )
```

```python
import functools

import jax
import jax.numpy as jnp
from jax import lax
from jax.experimental import pallas as pl
from jax.experimental.pallas import tpu as pltpu
from jax.sharding import Mesh
from jax.sharding import PartitionSpec as P

AXES = ("y", "z", "x", "core")
F32 = jnp.float32
BF16 = jnp.bfloat16
HIGHEST = lax.Precision.HIGHEST
CHUNKS = 4
stiffness = 1.0


def dot(a, b, contract=((1,), (0,)), precision=None):
    return lax.dot_general(a, b, (contract, ((), ())), precision=precision, preferred_element_type=F32)


def three_parts(values):
    upper = values.astype(BF16)
    rest = values - upper.astype(F32)
    middle = rest.astype(BF16)
    lower = (rest - middle.astype(F32)).astype(BF16)
    return upper, middle, lower


def two_parts(values):
    upper = values.astype(BF16)
    return upper, (values - upper.astype(F32)).astype(BF16)


def sweep_block(k, ref):
    n = ref.shape[0]
    b = BLOCK
    start = pl.multiple_of(k * b, b)
    lane = lax.broadcasted_iota(jnp.int32, (b, n), 1)
    row = lax.broadcasted_iota(jnp.int32, (b, n), 0)
    wide_lane = lax.broadcasted_iota(jnp.int32, (n, n), 1)
    panel = ref[pl.ds(start, b), :]
    turned = pltpu.roll(panel, lax.rem(n - start, n), axis=1)
    columns = [jnp.broadcast_to(turned[:, j : j + 1], (b, n)) for j in range(b)]
    inside = (lane >= start) & (lane < start + b)
    work = jnp.where(inside, jnp.where(lane - start == row, 1.0, 0.0), panel)
    for j in range(b):
        inv = 1.0 / jnp.broadcast_to(columns[j][j : j + 1, :], (b, n))
        factor = columns[j] * inv
        here = row == j

        def eliminated(value):
            pivot = jnp.broadcast_to(value[j : j + 1, :], (b, n))
            return jnp.where(here, pivot * inv, value - factor * pivot)

        for i in range(j + 1, b):
            columns[i] = eliminated(columns[i])
        work = eliminated(work)
    column = jnp.where(inside, 0.0, jnp.where(lane < start, -panel, panel))
    ch, cm, cl = three_parts(column)
    wh, wm, wl = three_parts(work)
    lhs = jnp.concatenate([ch, ch, cm, cm, ch, cl], axis=0)
    rhs = jnp.concatenate([wh, wm, wh, wm, wl, wh], axis=0)
    update = dot(lhs, rhs, ((0,), (0,)))
    outside = (wide_lane < start) | (wide_lane >= start + b)
    ref[...] = jnp.where(outside, ref[...], 0.0) - update
    ref[pl.ds(start, b), :] = work


def pack(matrix, ref):
    n = matrix.shape[0]
    half, count = n // 2, ref.shape[0]
    each = half // count
    matrix = 0.5 * (matrix + matrix.T)
    row = lax.broadcasted_iota(jnp.int32, (half, n), 0)
    lane = lax.broadcasted_iota(jnp.int32, (half, n), 1)
    upper = matrix[:half, :]
    turned = pltpu.roll(matrix[half:, :], half, axis=1)
    packed = jnp.where((lane < half) & (lane > row), turned, upper)
    diagonal = jnp.sum(jnp.where(lane == row, turned, 0.0), axis=0, keepdims=True)
    for s in range(count):
        ref[s, :each, :] = packed[s * each : (s + 1) * each, :]
        ref[s, each : each + 1, :] = diagonal


def unpack(ref):
    count, each, n = ref.shape
    each, half = each - 1, n // 2
    packed = jnp.concatenate([ref[s, :each, :] for s in range(count)], axis=0)
    diagonal = ref[0, each : each + 1, :]
    row = lax.broadcasted_iota(jnp.int32, (half, n), 0)
    lane = lax.broadcasted_iota(jnp.int32, (half, n), 1)
    turned = jnp.concatenate([packed, packed], axis=0).T
    upper = jnp.where((lane < half) & (lane > row), turned[:half, :], packed)
    lower = jnp.where(lane > row, packed, jnp.where(lane == row, diagonal, turned[:half, :]))
    lower = jnp.where(lane < half, turned[half:, :], pltpu.roll(lower, half, axis=1))
    return jnp.concatenate([upper, lower], axis=0)


def comm_kernel(
    ny, nz, nx, nc,
    op_hbm, rhs_hbm, size_ref, nbr_hbm, keep_hbm,
    live_ref, rounded_ref, image_ref, inverse_ref, rest_ref,
    op_ref, pt_ref, pm_ref, ahead_ref, behind_ref, right_ref, nbr_ref, keep_ref,
    cgram_ref, cxin_ref, cy_ref, cyin_ref, cz_ref, czin_ref, csum_ref,
    gram_ref, xin_ref, ychunk_ref, yin_ref, zown_ref, zin_ref, part_ref,
    y_known, z_known, in_sem, f_send, f_recv, b_send, b_recv,
    cxs, cxr, cys, cyr, czs, czr, cxs2, cxr2,
    xs, xr, ys, yr, zs, zr, ys2, yr2, xs2, xr2,
):
    y, z, x, core = (lax.axis_index(a) for a in AXES)
    clu = y * nz + z
    nclu = ny * nz
    nsub = nx * nc
    sub = x * nc + core
    nxt = lax.rem(clu + 1, nclu)
    prv = lax.rem(clu + nclu - 1, nclu)

    def at_clu(c):
        return (c // nz, lax.rem(c, nz), x, core)

    def at_sub(s):
        return (y, z, s // nc, lax.rem(s, nc))

    next_id, prev_id = at_clu(nxt), at_clu(prv)
    sub_ids = [None] + [at_sub(lax.rem(sub + d, nsub)) for d in range(1, nsub)]
    y_ids = [None] + [(lax.rem(y + d, ny), z, x, core) for d in range(1, ny)]
    z_ids = [None] + [(y, lax.rem(z + d, nz), x, core) for d in range(1, nz)]

    barrier = pltpu.get_barrier_semaphore()
    greeted = [next_id, prev_id, y_ids[1], y_ids[-1], z_ids[1], z_ids[-1]] + sub_ids[1:]

    def signal(semaphore, device):
        pl.semaphore_signal(semaphore, inc=1, device_id=device, device_id_type=pl.DeviceIdType.MESH)

    for device in greeted:
        signal(barrier, device)

    loads = [
        pltpu.make_async_copy(src, dst, in_sem.at[i])
        for i, (src, dst) in enumerate(
            [(rhs_hbm.at[0], live_ref), (keep_hbm, keep_ref), (nbr_hbm, nbr_ref), (op_hbm.at[0], op_ref)]
        )
    ]
    for load in loads:
        load.start()

    height, breadth = rounded_ref.shape
    step = height // CHUNKS
    size = size_ref[0]
    tiles = [pl.ds(t * step, step) for t in range(CHUNKS)]

    def remote(src, dst, send, recv, device):
        return pltpu.make_async_remote_copy(
            src_ref=src, dst_ref=dst, send_sem=send, recv_sem=recv,
            device_id=device, device_id_type=pl.DeviceIdType.MESH,
        )

    for load in loads[:3]:
        load.wait()
    keep = keep_ref[...].astype(F32)
    for t, rows in enumerate(tiles):
        index = lax.broadcasted_iota(jnp.int32, (step, breadth), 0) + t * step
        live = jnp.where(index < size, live_ref[rows, :], 0.0)
        live_ref[rows, :] = live
        rounded_ref[rows, :] = (live * keep).astype(BF16)
        index = lax.broadcasted_iota(jnp.int32, (step, height), 0) + t * step
        pt_ref[rows, :] = jnp.where(index == nbr_ref[...], 1.0, 0.0).astype(BF16)
    for rows in tiles:
        ahead_ref[rows, :] = dot(pt_ref[rows, :], rounded_ref[...]).astype(BF16)

    pl.semaphore_wait(barrier, len(greeted))

    forward, backward = [], []
    for t, rows in enumerate(tiles):
        forward.append(remote(rounded_ref.at[rows, :], behind_ref.at[rows, :], f_send.at[t], f_recv.at[t], next_id))
        backward.append(remote(ahead_ref.at[rows, :], right_ref.at[rows, :], b_send.at[t], b_recv.at[t], prev_id))
        forward[t].start()
        backward[t].start()

    tall = jnp.broadcast_to(nbr_ref[...].astype(F32), (breadth, height)).T
    for c in range(0, height, breadth):
        lanes = (lax.broadcasted_iota(jnp.int32, (height, breadth), 1) + c).astype(F32)
        pm_ref[:, c : c + breadth] = jnp.where(tall == lanes, 1.0, 0.0).astype(BF16)
    has_prev = clu > 0
    has_next = clu < nclu - 1
    degree = has_prev.astype(F32) + has_next.astype(F32)
    loads[3].wait()
    for rows in tiles:
        product = dot(op_ref[rows, :], rounded_ref[...])
        image_ref[rows, :] = product + stiffness * degree * rounded_ref[rows, :].astype(F32)

    for r in range(max(ny, nz) // 2 - 1):
        rings = [(known, ids) for known, ids, n in ((y_known, y_ids, ny), (z_known, z_ids, nz)) if r < n // 2 - 1]
        for known, ids in rings:
            signal(known.at[2 * r], ids[1])
            signal(known.at[2 * r + 1], ids[-1])
        for known, ids in rings:
            pl.semaphore_wait(known.at[2 * r], 1)
            pl.semaphore_wait(known.at[2 * r + 1], 1)

    prev_scale = jnp.where(has_prev, stiffness, 0.0).astype(F32)
    next_scale = jnp.where(has_next, stiffness, 0.0).astype(F32)
    for t, rows in enumerate(tiles):
        backward[t].wait_recv()
        image_ref[rows, :] = image_ref[rows, :] - next_scale * right_ref[rows, :].astype(F32)
        forward[t].wait_recv()
        if t < CHUNKS - 1:
            block = behind_ref[rows, :]
            for out in tiles:
                left = dot(pm_ref[out, rows], block)
                image_ref[out, :] = image_ref[out, :] - prev_scale * left
    block = behind_ref[tiles[-1], :]
    curvature = None
    for t, out in enumerate(tiles):
        left = dot(pm_ref[out, tiles[-1]], block)
        index = lax.broadcasted_iota(jnp.int32, (step, breadth), 0) + t * step
        image = jnp.where(index < size, image_ref[out, :] - prev_scale * left, 0.0)
        image_ref[out, :] = image
        term = dot(rounded_ref[out, :], jnp.concatenate(two_parts(image), axis=1), ((0,), (0,)))
        curvature = term if curvature is None else curvature + term
    curvature = curvature[:, :breadth] + curvature[:, breadth:]
    slab = breadth // nsub
    half = breadth // 2
    pack(curvature, cgram_ref)

    sent = []

    def whole(sources, landings, count, send, recv, ids):
        sent.append(remote(sources, sources, send, recv, ids[1]))
        return remote(landings, landings, send, recv, ids[1])

    def scatter(source, place, count, landing, send, recv, ids):
        for d in range(1, count):
            remote(source.at[lax.rem(place + d, count)], landing.at[d], send, recv, ids[d]).start()
        return whole(source.at[pl.ds(0, count - 1)], landing.at[pl.ds(1, count - 1)], count, send, recv, ids)

    def spread(source, count, landing, send, recv, ids):
        for d in range(1, count):
            remote(source, landing.at[d], send, recv, ids[d]).start()
        slots = landing.at[pl.ds(1, count - 1)]
        return whole(slots, slots, count, send, recv, ids)

    def share(array, place, count, send, recv, ids):
        for d in range(1, count):
            remote(array.at[place], array.at[place], send, recv, ids[d]).start()
        slots = array.at[pl.ds(0, count - 1)]
        return whole(slots, slots, count, send, recv, ids)

    def add_up(total, copies, landing):
        copies.wait_recv()
        for d in range(1, landing.shape[0]):
            total = total + landing[d]
        return total

    cx = scatter(cgram_ref, sub, nsub, cxin_ref, cxs, cxr, sub_ids)
    gram = None
    for out in tiles:
        ih, im = two_parts(image_ref[out, :])
        lh, lm = two_parts(live_ref[out, :])
        lhs = jnp.concatenate([rounded_ref[out, :], ih, im], axis=1)
        rhs = jnp.concatenate([lh, ih, lm, im], axis=1)
        term = dot(lhs, rhs, ((0,), (0,)))
        gram = term if gram is None else gram + term
    first = gram[: 2 * breadth, : 2 * breadth] + gram[: 2 * breadth, 2 * breadth :]
    second = first[breadth:, :] + gram[2 * breadth :, : 2 * breadth]
    others = (first[:breadth, :breadth], second[:, breadth:], second[:, :breadth])
    for s in range(nsub):
        for k, piece in enumerate(others):
            gram_ref[s, k * slab : (k + 1) * slab, :] = piece[s * slab : (s + 1) * slab, :]
    rx = scatter(gram_ref, sub, nsub, xin_ref, xs, xr, sub_ids)

    cy_ref[...] = add_up(cgram_ref[sub], cx, cxin_ref)
    cy = spread(cy_ref, ny, cyin_ref, cys, cyr, y_ids)
    total = add_up(gram_ref[sub], rx, xin_ref)
    rows_y = total.shape[0] // ny
    for v in range(ny):
        ychunk_ref[v] = total[v * rows_y : (v + 1) * rows_y, :]
    ry = scatter(ychunk_ref, y, ny, yin_ref, ys, yr, y_ids)

    cz_ref[...] = add_up(cy_ref[...], cy, cyin_ref)
    cz = spread(cz_ref, nz, czin_ref, czs, czr, z_ids)
    zown_ref[...] = add_up(ychunk_ref[y], ry, yin_ref)
    rz = spread(zown_ref, nz, zin_ref, zs, zr, z_ids)

    csum_ref[sub] = add_up(cz_ref[...], cz, czin_ref)
    cx2 = share(csum_ref, sub, nsub, cxs2, cxr2, sub_ids)
    part_ref[y] = add_up(zown_ref[...], rz, zin_ref)
    ry2 = share(part_ref, y, ny, ys2, yr2, y_ids)

    cx2.wait_recv()
    ry2.wait_recv()
    for v in range(ny):
        rest_ref[sub, v * rows_y : (v + 1) * rows_y, :] = part_ref[v]
    rx2 = share(rest_ref, sub, nsub, xs2, xr2, sub_ids)
    summed = unpack(csum_ref)
    rows = lax.broadcasted_iota(jnp.int32, (breadth, breadth), 0)
    lanes = lax.broadcasted_iota(jnp.int32, (breadth, breadth), 1)
    inverse_ref[...] = summed + jnp.where(rows == lanes, 1.0 - keep, 0.0)

    def sweep(first, last):
        def one(k, carry):
            sweep_block(k, inverse_ref)
            return carry

        lax.fori_loop(first, last, one, 0)

    blocks = breadth // BLOCK
    sweep(0, blocks)
    for copy in forward + backward + sent:
        copy.wait_send()
    rx2.wait_recv()


def hbm_only(array):
    return pltpu.with_memory_space_constraint(array, pltpu.HBM)


def communicate(operator, rhs, sizes, neighbours, kept, ny, nz, nx, nc):
    height, breadth = rhs.shape[1:]
    nsub = nx * nc
    slab = breadth // nsub
    piece = 3 * slab // ny
    packed = slab // 2 + 1
    signals = pltpu.SemaphoreType.REGULAR
    vmem = pl.BlockSpec(memory_space=pltpu.VMEM)
    hbm = pl.BlockSpec(memory_space=pltpu.HBM)
    dma = pltpu.SemaphoreType.DMA
    tall = (height, breadth)
    return pl.pallas_call(
        functools.partial(comm_kernel, ny, nz, nx, nc),
        name="exchange_and_sums",
        out_shape=(
            jax.ShapeDtypeStruct(tall, F32),
            jax.ShapeDtypeStruct(tall, BF16),
            jax.ShapeDtypeStruct(tall, F32),
            jax.ShapeDtypeStruct((breadth, breadth), F32),
            jax.ShapeDtypeStruct((nsub, 3 * slab, breadth), F32),
        ),
        in_specs=[hbm, hbm, pl.BlockSpec(memory_space=pltpu.SMEM), hbm, hbm],
        out_specs=(vmem,) * 5,
        scratch_shapes=[
            pltpu.VMEM((height, height), BF16),
            pltpu.VMEM((height, height), BF16),
            pltpu.VMEM((height, height), BF16),
            pltpu.VMEM(tall, BF16),
            pltpu.VMEM(tall, BF16),
            pltpu.VMEM(tall, BF16),
            pltpu.VMEM((1, height), jnp.int32),
            pltpu.VMEM((1, breadth), jnp.int32),
            pltpu.VMEM((nsub, packed, breadth), F32),
            pltpu.VMEM((nsub, packed, breadth), F32),
            pltpu.VMEM((packed, breadth), F32),
            pltpu.VMEM((ny, packed, breadth), F32),
            pltpu.VMEM((packed, breadth), F32),
            pltpu.VMEM((nz, packed, breadth), F32),
            pltpu.VMEM((nsub, packed, breadth), F32),
            pltpu.VMEM((nsub, 3 * slab, breadth), F32),
            pltpu.VMEM((nsub, 3 * slab, breadth), F32),
            pltpu.VMEM((ny, piece, breadth), F32),
            pltpu.VMEM((ny, piece, breadth), F32),
            pltpu.VMEM((piece, breadth), F32),
            pltpu.VMEM((nz, piece, breadth), F32),
            pltpu.VMEM((ny, piece, breadth), F32),
            signals((max(ny - 2, 2),)), signals((max(nz - 2, 2),)),
            dma((4,)),
            dma((CHUNKS,)), dma((CHUNKS,)), dma((CHUNKS,)), dma((CHUNKS,)),
            *[dma(())] * 18,
        ],
        compiler_params=pltpu.CompilerParams(
            collective_id=0, has_side_effects=True, vmem_limit_bytes=40 * 2**20
        ),
    )(hbm_only(operator), hbm_only(rhs), sizes, hbm_only(neighbours), hbm_only(kept))


BLOCK = 16


def update_kernel(
    live_ref, rounded_ref, image_ref, inverse_ref, rest_ref,
    solution_hbm, residual_hbm, direction_hbm,
    solution_ref, residual_ref, direction_ref, sems,
):
    nsub, rows3 = rest_ref.shape[:2]
    slab = rows3 // 3
    height = live_ref.shape[0]
    step = height // CHUNKS

    def matrix(k):
        return jnp.concatenate([rest_ref[s, k * slab : (k + 1) * slab, :] for s in range(nsub)], axis=0)

    inverse = inverse_ref[...]
    weights = dot(inverse, matrix(0), precision=HIGHEST)
    coupled = matrix(2) - dot(matrix(1), weights, precision=HIGHEST)
    correction = dot(inverse, coupled, precision=HIGHEST)
    wh, wm, wl = three_parts(weights)
    zh, zm, zl = three_parts(correction)
    n = weights.shape[0]
    wide = jnp.concatenate([wh, wm, wl, zh, zm, zl], axis=1)
    copies = []
    for t in range(CHUNKS):
        rows = pl.ds(t * step, step)
        live = live_ref[rows, :]
        spread = dot(rounded_ref[rows, :], wide)
        ih, im, il = three_parts(image_ref[rows, :])
        first = dot(ih, wide[:, : 3 * n])
        second = dot(im, wide[:, : 2 * n])
        third = dot(il, wh)
        moved = first[:, :n] + (first[:, n : 2 * n] + second[:, :n]) + (first[:, 2 * n :] + second[:, n:] + third)
        residual = live - moved
        solution_ref[rows, :] = spread[:, :n] + spread[:, n : 2 * n] + spread[:, 2 * n : 3 * n]
        residual_ref[rows, :] = residual
        direction_ref[rows, :] = residual - (
            spread[:, 3 * n : 4 * n] + spread[:, 4 * n : 5 * n] + spread[:, 5 * n :]
        )
        for k, (src, dst) in enumerate(
            [(solution_ref, solution_hbm), (residual_ref, residual_hbm), (direction_ref, direction_hbm)]
        ):
            copies.append(pltpu.make_async_copy(src.at[rows, :], dst.at[0, rows, :], sems.at[k, t]))
            copies[-1].start()
    for copy in copies:
        copy.wait()


def update(live, rounded, image, inverse, rest):
    vmem = pl.BlockSpec(memory_space=pltpu.VMEM)
    return pl.pallas_call(
        update_kernel,
        name="update",
        out_shape=[jax.ShapeDtypeStruct((1, *live.shape), F32)] * 3,
        in_specs=[vmem] * 5,
        out_specs=[pl.BlockSpec(memory_space=pltpu.HBM)] * 3,
        scratch_shapes=[pltpu.VMEM(live.shape, F32)] * 3 + [pltpu.SemaphoreType.DMA((3, CHUNKS))],
        compiler_params=pltpu.CompilerParams(vmem_limit_bytes=40 * 2**20),
    )(live, rounded, image, inverse, rest)


def per_device(ny, nz, nx, nc, operator, rhs, interface_sizes, neighbour_rows, kept_columns):
    results = communicate(operator, rhs, interface_sizes, neighbour_rows, kept_columns, ny, nz, nx, nc)
    return tuple(update(*results))


def solution(mesh, grid=(8, 12, 4, 2)):
    finer = Mesh(mesh.devices.reshape(grid), AXES)
    in_specs = (P(AXES, None, None), P(AXES, None, None), P(AXES), P(AXES, None), P())
    out_specs = (P(AXES, None, None),) * 3
    return jax.shard_map(
        functools.partial(per_device, *grid), mesh=finer, in_specs=in_specs, out_specs=out_specs, check_vma=False
    )
```

```python
import functools

import jax
import jax.numpy as jnp
from jax import lax
from jax.experimental import pallas as pl
from jax.experimental.pallas import tpu as pltpu
from jax.sharding import Mesh
from jax.sharding import PartitionSpec as P

AXES = ("y", "z", "x", "core")
F32 = jnp.float32
BF16 = jnp.bfloat16
HIGHEST = lax.Precision.HIGHEST
CHUNKS = 4
stiffness = 1.0


def dot(a, b, contract=((1,), (0,)), precision=None):
    return lax.dot_general(a, b, (contract, ((), ())), precision=precision, preferred_element_type=F32)


def three_parts(values):
    upper = values.astype(BF16)
    rest = values - upper.astype(F32)
    middle = rest.astype(BF16)
    lower = (rest - middle.astype(F32)).astype(BF16)
    return upper, middle, lower


def two_parts(values):
    upper = values.astype(BF16)
    return upper, (values - upper.astype(F32)).astype(BF16)


def sweep_block(k, ref):
    n = ref.shape[0]
    b = BLOCK
    start = pl.multiple_of(k * b, b)
    lane = lax.broadcasted_iota(jnp.int32, (b, n), 1)
    row = lax.broadcasted_iota(jnp.int32, (b, n), 0)
    wide_lane = lax.broadcasted_iota(jnp.int32, (n, n), 1)
    panel = ref[pl.ds(start, b), :]
    turned = pltpu.roll(panel, lax.rem(n - start, n), axis=1)
    columns = [jnp.broadcast_to(turned[:, j : j + 1], (b, n)) for j in range(b)]
    inside = (lane >= start) & (lane < start + b)
    work = jnp.where(inside, jnp.where(lane - start == row, 1.0, 0.0), panel)
    for j in range(b):
        inv = 1.0 / jnp.broadcast_to(columns[j][j : j + 1, :], (b, n))
        factor = columns[j] * inv
        here = row == j

        def eliminated(value):
            pivot = jnp.broadcast_to(value[j : j + 1, :], (b, n))
            return jnp.where(here, pivot * inv, value - factor * pivot)

        for i in range(j + 1, b):
            columns[i] = eliminated(columns[i])
        work = eliminated(work)
    column = jnp.where(inside, 0.0, jnp.where(lane < start, -panel, panel))
    ch, cm, cl = three_parts(column)
    wh, wm, wl = three_parts(work)
    lhs = jnp.concatenate([ch, ch, cm, cm, ch, cl], axis=0)
    rhs = jnp.concatenate([wh, wm, wh, wm, wl, wh], axis=0)
    update = dot(lhs, rhs, ((0,), (0,)))
    outside = (wide_lane < start) | (wide_lane >= start + b)
    ref[...] = jnp.where(outside, ref[...], 0.0) - update
    ref[pl.ds(start, b), :] = work


def pack(matrix, ref):
    n = matrix.shape[0]
    half, count = n // 2, ref.shape[0]
    each = half // count
    matrix = 0.5 * (matrix + matrix.T)
    row = lax.broadcasted_iota(jnp.int32, (half, n), 0)
    lane = lax.broadcasted_iota(jnp.int32, (half, n), 1)
    upper = matrix[:half, :]
    turned = pltpu.roll(matrix[half:, :], half, axis=1)
    packed = jnp.where((lane < half) & (lane > row), turned, upper)
    diagonal = jnp.sum(jnp.where(lane == row, turned, 0.0), axis=0, keepdims=True)
    for s in range(count):
        ref[s, :each, :] = packed[s * each : (s + 1) * each, :]
        ref[s, each : each + 1, :] = diagonal


def unpack(ref):
    count, each, n = ref.shape
    each, half = each - 1, n // 2
    packed = jnp.concatenate([ref[s, :each, :] for s in range(count)], axis=0)
    diagonal = ref[0, each : each + 1, :]
    row = lax.broadcasted_iota(jnp.int32, (half, n), 0)
    lane = lax.broadcasted_iota(jnp.int32, (half, n), 1)
    turned = jnp.concatenate([packed, packed], axis=0).T
    upper = jnp.where((lane < half) & (lane > row), turned[:half, :], packed)
    lower = jnp.where(lane > row, packed, jnp.where(lane == row, diagonal, turned[:half, :]))
    lower = jnp.where(lane < half, turned[half:, :], pltpu.roll(lower, half, axis=1))
    return jnp.concatenate([upper, lower], axis=0)


def far_first(count):
    return sorted(range(1, count), key=lambda d: -min(d, count - d))


def comm_kernel(
    ny, nz, nx, nc,
    op_hbm, rhs_hbm, size_ref, nbr_hbm, keep_hbm,
    live_ref, rounded_ref, image_ref, inverse_ref, rest_ref,
    op_ref, pt_ref, pm_ref, ahead_ref, behind_ref, right_ref, nbr_ref, keep_ref,
    cgram_ref, cxin_ref, cy_ref, cyin_ref, cz_ref, czin_ref, csum_ref,
    gram_ref, xin_ref, ychunk_ref, yin_ref, zown_ref, zin_ref, part_ref,
    y_known, z_known, in_sem, f_send, f_recv, b_send, b_recv,
    cxs, cxr, cys, cyr, czs, czr, cxs2, cxr2,
    xs, xr, ys, yr, zs, zr, ys2, yr2, xs2, xr2,
):
    y, z, x, core = (lax.axis_index(a) for a in AXES)
    clu = y * nz + z
    nclu = ny * nz
    nsub = nx * nc
    sub = x * nc + core
    nxt = lax.rem(clu + 1, nclu)
    prv = lax.rem(clu + nclu - 1, nclu)

    def at_clu(c):
        return (c // nz, lax.rem(c, nz), x, core)

    def at_sub(s):
        return (y, z, s // nc, lax.rem(s, nc))

    next_id, prev_id = at_clu(nxt), at_clu(prv)
    sub_ids = [None] + [at_sub(lax.rem(sub + d, nsub)) for d in range(1, nsub)]
    y_ids = [None] + [(lax.rem(y + d, ny), z, x, core) for d in range(1, ny)]
    z_ids = [None] + [(y, lax.rem(z + d, nz), x, core) for d in range(1, nz)]

    barrier = pltpu.get_barrier_semaphore()
    greeted = [next_id, prev_id, y_ids[1], y_ids[-1], z_ids[1], z_ids[-1]] + sub_ids[1:]

    def signal(semaphore, device):
        pl.semaphore_signal(semaphore, inc=1, device_id=device, device_id_type=pl.DeviceIdType.MESH)

    for device in greeted:
        signal(barrier, device)

    loads = [
        pltpu.make_async_copy(src, dst, in_sem.at[i])
        for i, (src, dst) in enumerate(
            [(rhs_hbm.at[0], live_ref), (keep_hbm, keep_ref), (nbr_hbm, nbr_ref), (op_hbm.at[0], op_ref)]
        )
    ]
    for load in loads:
        load.start()

    height, breadth = rounded_ref.shape
    step = height // CHUNKS
    size = size_ref[0]
    tiles = [pl.ds(t * step, step) for t in range(CHUNKS)]

    def remote(src, dst, send, recv, device):
        return pltpu.make_async_remote_copy(
            src_ref=src, dst_ref=dst, send_sem=send, recv_sem=recv,
            device_id=device, device_id_type=pl.DeviceIdType.MESH,
        )

    for load in loads[:3]:
        load.wait()
    keep = keep_ref[...].astype(F32)
    for t, rows in enumerate(tiles):
        index = lax.broadcasted_iota(jnp.int32, (step, breadth), 0) + t * step
        live = jnp.where(index < size, live_ref[rows, :], 0.0)
        live_ref[rows, :] = live
        rounded_ref[rows, :] = (live * keep).astype(BF16)
        index = lax.broadcasted_iota(jnp.int32, (step, height), 0) + t * step
        pt_ref[rows, :] = jnp.where(index == nbr_ref[...], 1.0, 0.0).astype(BF16)
    for rows in tiles:
        ahead_ref[rows, :] = dot(pt_ref[rows, :], rounded_ref[...]).astype(BF16)

    pl.semaphore_wait(barrier, len(greeted))

    forward, backward = [], []
    for t, rows in enumerate(tiles):
        forward.append(remote(rounded_ref.at[rows, :], behind_ref.at[rows, :], f_send.at[t], f_recv.at[t], next_id))
        backward.append(remote(ahead_ref.at[rows, :], right_ref.at[rows, :], b_send.at[t], b_recv.at[t], prev_id))
        forward[t].start()
        backward[t].start()

    tall = jnp.broadcast_to(nbr_ref[...].astype(F32), (breadth, height)).T
    for c in range(0, height, breadth):
        lanes = (lax.broadcasted_iota(jnp.int32, (height, breadth), 1) + c).astype(F32)
        pm_ref[:, c : c + breadth] = jnp.where(tall == lanes, 1.0, 0.0).astype(BF16)
    has_prev = clu > 0
    has_next = clu < nclu - 1
    degree = has_prev.astype(F32) + has_next.astype(F32)
    loads[3].wait()
    for rows in tiles:
        product = dot(op_ref[rows, :], rounded_ref[...])
        image_ref[rows, :] = product + stiffness * degree * rounded_ref[rows, :].astype(F32)

    for r in range(max(ny, nz) // 2 - 1):
        rings = [(known, ids) for known, ids, n in ((y_known, y_ids, ny), (z_known, z_ids, nz)) if r < n // 2 - 1]
        for known, ids in rings:
            signal(known.at[2 * r], ids[1])
            signal(known.at[2 * r + 1], ids[-1])
        for known, ids in rings:
            pl.semaphore_wait(known.at[2 * r], 1)
            pl.semaphore_wait(known.at[2 * r + 1], 1)

    prev_scale = jnp.where(has_prev, stiffness, 0.0).astype(F32)
    next_scale = jnp.where(has_next, stiffness, 0.0).astype(F32)
    for t, rows in enumerate(tiles):
        backward[t].wait_recv()
        image_ref[rows, :] = image_ref[rows, :] - next_scale * right_ref[rows, :].astype(F32)
        forward[t].wait_recv()
        if t < CHUNKS - 1:
            block = behind_ref[rows, :]
            for out in tiles:
                left = dot(pm_ref[out, rows], block)
                image_ref[out, :] = image_ref[out, :] - prev_scale * left
    block = behind_ref[tiles[-1], :]
    curvature = None
    for t, out in enumerate(tiles):
        left = dot(pm_ref[out, tiles[-1]], block)
        index = lax.broadcasted_iota(jnp.int32, (step, breadth), 0) + t * step
        image = jnp.where(index < size, image_ref[out, :] - prev_scale * left, 0.0)
        image_ref[out, :] = image
        term = dot(rounded_ref[out, :], jnp.concatenate(two_parts(image), axis=1), ((0,), (0,)))
        curvature = term if curvature is None else curvature + term
    curvature = curvature[:, :breadth] + curvature[:, breadth:]
    slab = breadth // nsub
    half = breadth // 2
    pack(curvature, cgram_ref)

    sent = []

    def whole(sources, landings, count, send, recv, ids):
        sent.append(remote(sources, sources, send, recv, ids[1]))
        return remote(landings, landings, send, recv, ids[1])

    def scatter(source, place, count, landing, send, recv, ids):
        for d in far_first(count):
            remote(source.at[lax.rem(place + d, count)], landing.at[d], send, recv, ids[d]).start()
        return whole(source.at[pl.ds(0, count - 1)], landing.at[pl.ds(1, count - 1)], count, send, recv, ids)

    def spread(source, count, landing, send, recv, ids):
        for d in far_first(count):
            remote(source, landing.at[d], send, recv, ids[d]).start()
        slots = landing.at[pl.ds(1, count - 1)]
        return whole(slots, slots, count, send, recv, ids)

    def share(array, place, count, send, recv, ids):
        for d in far_first(count):
            remote(array.at[place], array.at[place], send, recv, ids[d]).start()
        slots = array.at[pl.ds(0, count - 1)]
        return whole(slots, slots, count, send, recv, ids)

    def add_up(total, copies, landing):
        copies.wait_recv()
        for d in range(1, landing.shape[0]):
            total = total + landing[d]
        return total

    cx = scatter(cgram_ref, sub, nsub, cxin_ref, cxs, cxr, sub_ids)
    gram = None
    for out in tiles:
        ih, im = two_parts(image_ref[out, :])
        lh, lm = two_parts(live_ref[out, :])
        lhs = jnp.concatenate([rounded_ref[out, :], ih, im], axis=1)
        rhs = jnp.concatenate([lh, ih, lm, im], axis=1)
        term = dot(lhs, rhs, ((0,), (0,)))
        gram = term if gram is None else gram + term
    first = gram[: 2 * breadth, : 2 * breadth] + gram[: 2 * breadth, 2 * breadth :]
    second = first[breadth:, :] + gram[2 * breadth :, : 2 * breadth]
    others = (first[:breadth, :breadth], second[:, breadth:], second[:, :breadth])
    for s in range(nsub):
        for k, piece in enumerate(others):
            gram_ref[s, k * slab : (k + 1) * slab, :] = piece[s * slab : (s + 1) * slab, :]
    rx = scatter(gram_ref, sub, nsub, xin_ref, xs, xr, sub_ids)

    cy_ref[...] = add_up(cgram_ref[sub], cx, cxin_ref)
    cy = spread(cy_ref, ny, cyin_ref, cys, cyr, y_ids)
    total = add_up(gram_ref[sub], rx, xin_ref)
    rows_y = total.shape[0] // ny
    for v in range(ny):
        ychunk_ref[v] = total[v * rows_y : (v + 1) * rows_y, :]
    ry = scatter(ychunk_ref, y, ny, yin_ref, ys, yr, y_ids)

    cz_ref[...] = add_up(cy_ref[...], cy, cyin_ref)
    cz = spread(cz_ref, nz, czin_ref, czs, czr, z_ids)
    zown_ref[...] = add_up(ychunk_ref[y], ry, yin_ref)
    rz = spread(zown_ref, nz, zin_ref, zs, zr, z_ids)

    csum_ref[sub] = add_up(cz_ref[...], cz, czin_ref)
    cx2 = share(csum_ref, sub, nsub, cxs2, cxr2, sub_ids)
    part_ref[y] = add_up(zown_ref[...], rz, zin_ref)
    ry2 = share(part_ref, y, ny, ys2, yr2, y_ids)

    cx2.wait_recv()
    ry2.wait_recv()
    for v in range(ny):
        rest_ref[sub, v * rows_y : (v + 1) * rows_y, :] = part_ref[v]
    rx2 = share(rest_ref, sub, nsub, xs2, xr2, sub_ids)
    summed = unpack(csum_ref)
    rows = lax.broadcasted_iota(jnp.int32, (breadth, breadth), 0)
    lanes = lax.broadcasted_iota(jnp.int32, (breadth, breadth), 1)
    inverse_ref[...] = summed + jnp.where(rows == lanes, 1.0 - keep, 0.0)

    def sweep(first, last):
        def one(k, carry):
            sweep_block(k, inverse_ref)
            return carry

        lax.fori_loop(first, last, one, 0)

    blocks = breadth // BLOCK
    sweep(0, blocks)
    for copy in forward + backward + sent:
        copy.wait_send()
    rx2.wait_recv()


def hbm_only(array):
    return pltpu.with_memory_space_constraint(array, pltpu.HBM)


def communicate(operator, rhs, sizes, neighbours, kept, ny, nz, nx, nc):
    height, breadth = rhs.shape[1:]
    nsub = nx * nc
    slab = breadth // nsub
    piece = 3 * slab // ny
    packed = slab // 2 + 1
    signals = pltpu.SemaphoreType.REGULAR
    vmem = pl.BlockSpec(memory_space=pltpu.VMEM)
    hbm = pl.BlockSpec(memory_space=pltpu.HBM)
    dma = pltpu.SemaphoreType.DMA
    tall = (height, breadth)
    return pl.pallas_call(
        functools.partial(comm_kernel, ny, nz, nx, nc),
        name="exchange_and_sums",
        out_shape=(
            jax.ShapeDtypeStruct(tall, F32),
            jax.ShapeDtypeStruct(tall, BF16),
            jax.ShapeDtypeStruct(tall, F32),
            jax.ShapeDtypeStruct((breadth, breadth), F32),
            jax.ShapeDtypeStruct((nsub, 3 * slab, breadth), F32),
        ),
        in_specs=[hbm, hbm, pl.BlockSpec(memory_space=pltpu.SMEM), hbm, hbm],
        out_specs=(vmem,) * 5,
        scratch_shapes=[
            pltpu.VMEM((height, height), BF16),
            pltpu.VMEM((height, height), BF16),
            pltpu.VMEM((height, height), BF16),
            pltpu.VMEM(tall, BF16),
            pltpu.VMEM(tall, BF16),
            pltpu.VMEM(tall, BF16),
            pltpu.VMEM((1, height), jnp.int32),
            pltpu.VMEM((1, breadth), jnp.int32),
            pltpu.VMEM((nsub, packed, breadth), F32),
            pltpu.VMEM((nsub, packed, breadth), F32),
            pltpu.VMEM((packed, breadth), F32),
            pltpu.VMEM((ny, packed, breadth), F32),
            pltpu.VMEM((packed, breadth), F32),
            pltpu.VMEM((nz, packed, breadth), F32),
            pltpu.VMEM((nsub, packed, breadth), F32),
            pltpu.VMEM((nsub, 3 * slab, breadth), F32),
            pltpu.VMEM((nsub, 3 * slab, breadth), F32),
            pltpu.VMEM((ny, piece, breadth), F32),
            pltpu.VMEM((ny, piece, breadth), F32),
            pltpu.VMEM((piece, breadth), F32),
            pltpu.VMEM((nz, piece, breadth), F32),
            pltpu.VMEM((ny, piece, breadth), F32),
            signals((max(ny - 2, 2),)), signals((max(nz - 2, 2),)),
            dma((4,)),
            dma((CHUNKS,)), dma((CHUNKS,)), dma((CHUNKS,)), dma((CHUNKS,)),
            *[dma(())] * 18,
        ],
        compiler_params=pltpu.CompilerParams(
            collective_id=0, has_side_effects=True, vmem_limit_bytes=40 * 2**20
        ),
    )(hbm_only(operator), hbm_only(rhs), sizes, hbm_only(neighbours), hbm_only(kept))


BLOCK = 16


def update_kernel(
    live_ref, rounded_ref, image_ref, inverse_ref, rest_ref,
    solution_hbm, residual_hbm, direction_hbm,
    solution_ref, residual_ref, direction_ref, sems,
):
    nsub, rows3 = rest_ref.shape[:2]
    slab = rows3 // 3
    height = live_ref.shape[0]
    step = height // CHUNKS

    def matrix(k):
        return jnp.concatenate([rest_ref[s, k * slab : (k + 1) * slab, :] for s in range(nsub)], axis=0)

    inverse = inverse_ref[...]
    weights = dot(inverse, matrix(0), precision=HIGHEST)
    coupled = matrix(2) - dot(matrix(1), weights, precision=HIGHEST)
    correction = dot(inverse, coupled, precision=HIGHEST)
    wh, wm, wl = three_parts(weights)
    zh, zm, zl = three_parts(correction)
    n = weights.shape[0]
    wide = jnp.concatenate([wh, wm, wl, zh, zm, zl], axis=1)
    copies = []
    for t in range(CHUNKS):
        rows = pl.ds(t * step, step)
        live = live_ref[rows, :]
        spread = dot(rounded_ref[rows, :], wide)
        ih, im, il = three_parts(image_ref[rows, :])
        first = dot(ih, wide[:, : 3 * n])
        second = dot(im, wide[:, : 2 * n])
        third = dot(il, wh)
        moved = first[:, :n] + (first[:, n : 2 * n] + second[:, :n]) + (first[:, 2 * n :] + second[:, n:] + third)
        residual = live - moved
        solution_ref[rows, :] = spread[:, :n] + spread[:, n : 2 * n] + spread[:, 2 * n : 3 * n]
        residual_ref[rows, :] = residual
        direction_ref[rows, :] = residual - (
            spread[:, 3 * n : 4 * n] + spread[:, 4 * n : 5 * n] + spread[:, 5 * n :]
        )
        for k, (src, dst) in enumerate(
            [(solution_ref, solution_hbm), (residual_ref, residual_hbm), (direction_ref, direction_hbm)]
        ):
            copies.append(pltpu.make_async_copy(src.at[rows, :], dst.at[0, rows, :], sems.at[k, t]))
            copies[-1].start()
    for copy in copies:
        copy.wait()


def update(live, rounded, image, inverse, rest):
    vmem = pl.BlockSpec(memory_space=pltpu.VMEM)
    return pl.pallas_call(
        update_kernel,
        name="update",
        out_shape=[jax.ShapeDtypeStruct((1, *live.shape), F32)] * 3,
        in_specs=[vmem] * 5,
        out_specs=[pl.BlockSpec(memory_space=pltpu.HBM)] * 3,
        scratch_shapes=[pltpu.VMEM(live.shape, F32)] * 3 + [pltpu.SemaphoreType.DMA((3, CHUNKS))],
        compiler_params=pltpu.CompilerParams(vmem_limit_bytes=40 * 2**20),
    )(live, rounded, image, inverse, rest)


def per_device(ny, nz, nx, nc, operator, rhs, interface_sizes, neighbour_rows, kept_columns):
    results = communicate(operator, rhs, interface_sizes, neighbour_rows, kept_columns, ny, nz, nx, nc)
    return tuple(update(*results))


def solution(mesh, grid=(8, 12, 4, 2)):
    finer = Mesh(mesh.devices.reshape(grid), AXES)
    in_specs = (P(AXES, None, None), P(AXES, None, None), P(AXES), P(AXES, None), P())
    out_specs = (P(AXES, None, None),) * 3
    return jax.shard_map(
        functools.partial(per_device, *grid), mesh=finer, in_specs=in_specs, out_specs=out_specs, check_vma=False
    )
```

```python
import functools

import jax
import jax.numpy as jnp
from jax import lax
from jax.experimental import pallas as pl
from jax.experimental.pallas import tpu as pltpu
from jax.sharding import Mesh
from jax.sharding import PartitionSpec as P

AXES = ("y", "z", "x", "core")
F32 = jnp.float32
BF16 = jnp.bfloat16
HIGHEST = lax.Precision.HIGHEST
CHUNKS = 4
stiffness = 1.0


def dot(a, b, contract=((1,), (0,)), precision=None):
    return lax.dot_general(a, b, (contract, ((), ())), precision=precision, preferred_element_type=F32)


def three_parts(values):
    upper = values.astype(BF16)
    rest = values - upper.astype(F32)
    middle = rest.astype(BF16)
    lower = (rest - middle.astype(F32)).astype(BF16)
    return upper, middle, lower


def two_parts(values):
    upper = values.astype(BF16)
    return upper, (values - upper.astype(F32)).astype(BF16)


def sweep_block(k, ref):
    n = ref.shape[0]
    b = BLOCK
    start = k * b
    lane = lax.broadcasted_iota(jnp.int32, (b, n), 1)
    row = lax.broadcasted_iota(jnp.int32, (b, n), 0)
    wide_lane = lax.broadcasted_iota(jnp.int32, (n, n), 1)
    panel = ref[pl.ds(start, b), :]
    turned = panel
    columns = [jnp.broadcast_to(turned[:, start + j : start + j + 1], (b, n)) for j in range(b)]
    inside = (lane >= start) & (lane < start + b)
    work = jnp.where(inside, jnp.where(lane - start == row, 1.0, 0.0), panel)
    for j in range(b):
        inv = 1.0 / jnp.broadcast_to(columns[j][j : j + 1, :], (b, n))
        factor = columns[j] * inv
        here = row == j

        def eliminated(value):
            pivot = jnp.broadcast_to(value[j : j + 1, :], (b, n))
            return jnp.where(here, pivot * inv, value - factor * pivot)

        for i in range(j + 1, b):
            columns[i] = eliminated(columns[i])
        work = eliminated(work)
    column = jnp.where(inside, 0.0, jnp.where(lane < start, -panel, panel))
    ch, cm, cl = three_parts(column)
    wh, wm, wl = three_parts(work)
    lhs = jnp.concatenate([ch, ch, cm, cm, ch, cl], axis=0)
    rhs = jnp.concatenate([wh, wm, wh, wm, wl, wh], axis=0)
    update = dot(lhs, rhs, ((0,), (0,)))
    outside = (wide_lane < start) | (wide_lane >= start + b)
    ref[...] = jnp.where(outside, ref[...], 0.0) - update
    ref[pl.ds(start, b), :] = work


def pack(matrix, ref):
    n = matrix.shape[0]
    half, count = n // 2, ref.shape[0]
    each = half // count
    matrix = 0.5 * (matrix + matrix.T)
    row = lax.broadcasted_iota(jnp.int32, (half, n), 0)
    lane = lax.broadcasted_iota(jnp.int32, (half, n), 1)
    upper = matrix[:half, :]
    turned = pltpu.roll(matrix[half:, :], half, axis=1)
    packed = jnp.where((lane < half) & (lane > row), turned, upper)
    diagonal = jnp.sum(jnp.where(lane == row, turned, 0.0), axis=0, keepdims=True)
    for s in range(count):
        ref[s, :each, :] = packed[s * each : (s + 1) * each, :]
        ref[s, each : each + 1, :] = diagonal


def unpack(ref):
    count, each, n = ref.shape
    each, half = each - 1, n // 2
    packed = jnp.concatenate([ref[s, :each, :] for s in range(count)], axis=0)
    diagonal = ref[0, each : each + 1, :]
    row = lax.broadcasted_iota(jnp.int32, (half, n), 0)
    lane = lax.broadcasted_iota(jnp.int32, (half, n), 1)
    turned = jnp.concatenate([packed, packed], axis=0).T
    upper = jnp.where((lane < half) & (lane > row), turned[:half, :], packed)
    lower = jnp.where(lane > row, packed, jnp.where(lane == row, diagonal, turned[:half, :]))
    lower = jnp.where(lane < half, turned[half:, :], pltpu.roll(lower, half, axis=1))
    return jnp.concatenate([upper, lower], axis=0)


def far_first(count):
    return sorted(range(1, count), key=lambda d: -min(d, count - d))


def comm_kernel(
    ny, nz, nx, nc,
    op_hbm, rhs_hbm, size_ref, nbr_hbm, keep_hbm,
    live_ref, rounded_ref, image_ref, inverse_ref, rest_ref,
    op_ref, pt_ref, pm_ref, ahead_ref, behind_ref, right_ref, nbr_ref, keep_ref,
    cgram_ref, cxin_ref, cy_ref, cyin_ref, cz_ref, czin_ref, csum_ref,
    gram_ref, xin_ref, ychunk_ref, yin_ref, zown_ref, zin_ref, part_ref,
    y_known, z_known, in_sem, f_send, f_recv, b_send, b_recv,
    cxs, cxr, cys, cyr, czs, czr, cxs2, cxr2,
    xs, xr, ys, yr, zs, zr, ys2, yr2, xs2, xr2,
):
    y, z, x, core = (lax.axis_index(a) for a in AXES)
    clu = y * nz + z
    nclu = ny * nz
    nsub = nx * nc
    sub = x * nc + core
    nxt = lax.rem(clu + 1, nclu)
    prv = lax.rem(clu + nclu - 1, nclu)

    def at_clu(c):
        return (c // nz, lax.rem(c, nz), x, core)

    def at_sub(s):
        return (y, z, s // nc, lax.rem(s, nc))

    next_id, prev_id = at_clu(nxt), at_clu(prv)
    sub_ids = [None] + [at_sub(lax.rem(sub + d, nsub)) for d in range(1, nsub)]
    y_ids = [None] + [(lax.rem(y + d, ny), z, x, core) for d in range(1, ny)]
    z_ids = [None] + [(y, lax.rem(z + d, nz), x, core) for d in range(1, nz)]

    barrier = pltpu.get_barrier_semaphore()
    greeted = [next_id, prev_id, y_ids[1], y_ids[-1], z_ids[1], z_ids[-1]] + sub_ids[1:]

    def signal(semaphore, device):
        pl.semaphore_signal(semaphore, inc=1, device_id=device, device_id_type=pl.DeviceIdType.MESH)

    for device in greeted:
        signal(barrier, device)

    loads = [
        pltpu.make_async_copy(src, dst, in_sem.at[i])
        for i, (src, dst) in enumerate(
            [(rhs_hbm.at[0], live_ref), (keep_hbm, keep_ref), (nbr_hbm, nbr_ref), (op_hbm.at[0], op_ref)]
        )
    ]
    for load in loads:
        load.start()

    height, breadth = rounded_ref.shape
    step = height // CHUNKS
    size = size_ref[0]
    tiles = [pl.ds(t * step, step) for t in range(CHUNKS)]

    def remote(src, dst, send, recv, device):
        return pltpu.make_async_remote_copy(
            src_ref=src, dst_ref=dst, send_sem=send, recv_sem=recv,
            device_id=device, device_id_type=pl.DeviceIdType.MESH,
        )

    for load in loads[:3]:
        load.wait()
    keep = keep_ref[...].astype(F32)
    for t, rows in enumerate(tiles):
        index = lax.broadcasted_iota(jnp.int32, (step, breadth), 0) + t * step
        live = jnp.where(index < size, live_ref[rows, :], 0.0)
        live_ref[rows, :] = live
        rounded_ref[rows, :] = (live * keep).astype(BF16)
        index = lax.broadcasted_iota(jnp.int32, (step, height), 0) + t * step
        pt_ref[rows, :] = jnp.where(index == nbr_ref[...], 1.0, 0.0).astype(BF16)
    for rows in tiles:
        ahead_ref[rows, :] = dot(pt_ref[rows, :], rounded_ref[...]).astype(BF16)

    pl.semaphore_wait(barrier, len(greeted))

    forward, backward = [], []
    for t, rows in enumerate(tiles):
        forward.append(remote(rounded_ref.at[rows, :], behind_ref.at[rows, :], f_send.at[t], f_recv.at[t], next_id))
        backward.append(remote(ahead_ref.at[rows, :], right_ref.at[rows, :], b_send.at[t], b_recv.at[t], prev_id))
        forward[t].start()
        backward[t].start()

    tall = jnp.broadcast_to(nbr_ref[...].astype(F32), (breadth, height)).T
    for c in range(0, height, breadth):
        lanes = (lax.broadcasted_iota(jnp.int32, (height, breadth), 1) + c).astype(F32)
        pm_ref[:, c : c + breadth] = jnp.where(tall == lanes, 1.0, 0.0).astype(BF16)
    has_prev = clu > 0
    has_next = clu < nclu - 1
    degree = has_prev.astype(F32) + has_next.astype(F32)
    loads[3].wait()
    for rows in tiles:
        product = dot(op_ref[rows, :], rounded_ref[...])
        image_ref[rows, :] = product + stiffness * degree * rounded_ref[rows, :].astype(F32)

    for r in range(max(ny, nz) // 2 - 1):
        rings = [(known, ids) for known, ids, n in ((y_known, y_ids, ny), (z_known, z_ids, nz)) if r < n // 2 - 1]
        for known, ids in rings:
            signal(known.at[2 * r], ids[1])
            signal(known.at[2 * r + 1], ids[-1])
        for known, ids in rings:
            pl.semaphore_wait(known.at[2 * r], 1)
            pl.semaphore_wait(known.at[2 * r + 1], 1)

    prev_scale = jnp.where(has_prev, stiffness, 0.0).astype(F32)
    next_scale = jnp.where(has_next, stiffness, 0.0).astype(F32)
    for t, rows in enumerate(tiles):
        backward[t].wait_recv()
        image_ref[rows, :] = image_ref[rows, :] - next_scale * right_ref[rows, :].astype(F32)
        forward[t].wait_recv()
        if t < CHUNKS - 1:
            block = behind_ref[rows, :]
            for out in tiles:
                left = dot(pm_ref[out, rows], block)
                image_ref[out, :] = image_ref[out, :] - prev_scale * left
    block = behind_ref[tiles[-1], :]
    curvature = None
    for t, out in enumerate(tiles):
        left = dot(pm_ref[out, tiles[-1]], block)
        index = lax.broadcasted_iota(jnp.int32, (step, breadth), 0) + t * step
        image = jnp.where(index < size, image_ref[out, :] - prev_scale * left, 0.0)
        image_ref[out, :] = image
        term = dot(rounded_ref[out, :], jnp.concatenate(two_parts(image), axis=1), ((0,), (0,)))
        curvature = term if curvature is None else curvature + term
    curvature = curvature[:, :breadth] + curvature[:, breadth:]
    slab = breadth // nsub
    half = breadth // 2
    pack(curvature, cgram_ref)

    sent = []

    def whole(sources, landings, count, send, recv, ids):
        sent.append(remote(sources, sources, send, recv, ids[1]))
        return remote(landings, landings, send, recv, ids[1])

    def scatter(source, place, count, landing, send, recv, ids):
        for d in far_first(count):
            remote(source.at[lax.rem(place + d, count)], landing.at[d], send, recv, ids[d]).start()
        return whole(source.at[pl.ds(0, count - 1)], landing.at[pl.ds(1, count - 1)], count, send, recv, ids)

    def spread(source, count, landing, send, recv, ids):
        for d in far_first(count):
            remote(source, landing.at[d], send, recv, ids[d]).start()
        slots = landing.at[pl.ds(1, count - 1)]
        return whole(slots, slots, count, send, recv, ids)

    def share(array, place, count, send, recv, ids):
        for d in far_first(count):
            remote(array.at[place], array.at[place], send, recv, ids[d]).start()
        slots = array.at[pl.ds(0, count - 1)]
        return whole(slots, slots, count, send, recv, ids)

    def add_up(total, copies, landing):
        copies.wait_recv()
        for d in range(1, landing.shape[0]):
            total = total + landing[d]
        return total

    cx = scatter(cgram_ref, sub, nsub, cxin_ref, cxs, cxr, sub_ids)
    gram = None
    for out in tiles:
        ih, im = two_parts(image_ref[out, :])
        lh, lm = two_parts(live_ref[out, :])
        lhs = jnp.concatenate([rounded_ref[out, :], ih, im], axis=1)
        rhs = jnp.concatenate([lh, ih, lm, im], axis=1)
        term = dot(lhs, rhs, ((0,), (0,)))
        gram = term if gram is None else gram + term
    first = gram[: 2 * breadth, : 2 * breadth] + gram[: 2 * breadth, 2 * breadth :]
    second = first[breadth:, :] + gram[2 * breadth :, : 2 * breadth]
    others = (first[:breadth, :breadth], second[:, breadth:], second[:, :breadth])
    for s in range(nsub):
        for k, piece in enumerate(others):
            gram_ref[s, k * slab : (k + 1) * slab, :] = piece[s * slab : (s + 1) * slab, :]
    rx = scatter(gram_ref, sub, nsub, xin_ref, xs, xr, sub_ids)

    cy_ref[...] = add_up(cgram_ref[sub], cx, cxin_ref)
    cy = spread(cy_ref, ny, cyin_ref, cys, cyr, y_ids)
    total = add_up(gram_ref[sub], rx, xin_ref)
    rows_y = total.shape[0] // ny
    for v in range(ny):
        ychunk_ref[v] = total[v * rows_y : (v + 1) * rows_y, :]
    ry = scatter(ychunk_ref, y, ny, yin_ref, ys, yr, y_ids)

    cz_ref[...] = add_up(cy_ref[...], cy, cyin_ref)
    cz = spread(cz_ref, nz, czin_ref, czs, czr, z_ids)
    zown_ref[...] = add_up(ychunk_ref[y], ry, yin_ref)
    rz = spread(zown_ref, nz, zin_ref, zs, zr, z_ids)

    csum_ref[sub] = add_up(cz_ref[...], cz, czin_ref)
    cx2 = share(csum_ref, sub, nsub, cxs2, cxr2, sub_ids)
    part_ref[y] = add_up(zown_ref[...], rz, zin_ref)
    ry2 = share(part_ref, y, ny, ys2, yr2, y_ids)

    cx2.wait_recv()
    ry2.wait_recv()
    for v in range(ny):
        rest_ref[sub, v * rows_y : (v + 1) * rows_y, :] = part_ref[v]
    rx2 = share(rest_ref, sub, nsub, xs2, xr2, sub_ids)
    summed = unpack(csum_ref)
    rows = lax.broadcasted_iota(jnp.int32, (breadth, breadth), 0)
    lanes = lax.broadcasted_iota(jnp.int32, (breadth, breadth), 1)
    inverse_ref[...] = summed + jnp.where(rows == lanes, 1.0 - keep, 0.0)

    def sweep(first, last):
        def one(k, carry):
            sweep_block(k, inverse_ref)
            return carry

        for k in range(first, last):
            one(k, 0)

    blocks = breadth // BLOCK
    sweep(0, blocks)
    for copy in forward + backward + sent:
        copy.wait_send()
    rx2.wait_recv()


def hbm_only(array):
    return pltpu.with_memory_space_constraint(array, pltpu.HBM)


def communicate(operator, rhs, sizes, neighbours, kept, ny, nz, nx, nc):
    height, breadth = rhs.shape[1:]
    nsub = nx * nc
    slab = breadth // nsub
    piece = 3 * slab // ny
    packed = slab // 2 + 1
    signals = pltpu.SemaphoreType.REGULAR
    vmem = pl.BlockSpec(memory_space=pltpu.VMEM)
    hbm = pl.BlockSpec(memory_space=pltpu.HBM)
    dma = pltpu.SemaphoreType.DMA
    tall = (height, breadth)
    return pl.pallas_call(
        functools.partial(comm_kernel, ny, nz, nx, nc),
        name="exchange_and_sums",
        out_shape=(
            jax.ShapeDtypeStruct(tall, F32),
            jax.ShapeDtypeStruct(tall, BF16),
            jax.ShapeDtypeStruct(tall, F32),
            jax.ShapeDtypeStruct((breadth, breadth), F32),
            jax.ShapeDtypeStruct((nsub, 3 * slab, breadth), F32),
        ),
        in_specs=[hbm, hbm, pl.BlockSpec(memory_space=pltpu.SMEM), hbm, hbm],
        out_specs=(vmem,) * 5,
        scratch_shapes=[
            pltpu.VMEM((height, height), BF16),
            pltpu.VMEM((height, height), BF16),
            pltpu.VMEM((height, height), BF16),
            pltpu.VMEM(tall, BF16),
            pltpu.VMEM(tall, BF16),
            pltpu.VMEM(tall, BF16),
            pltpu.VMEM((1, height), jnp.int32),
            pltpu.VMEM((1, breadth), jnp.int32),
            pltpu.VMEM((nsub, packed, breadth), F32),
            pltpu.VMEM((nsub, packed, breadth), F32),
            pltpu.VMEM((packed, breadth), F32),
            pltpu.VMEM((ny, packed, breadth), F32),
            pltpu.VMEM((packed, breadth), F32),
            pltpu.VMEM((nz, packed, breadth), F32),
            pltpu.VMEM((nsub, packed, breadth), F32),
            pltpu.VMEM((nsub, 3 * slab, breadth), F32),
            pltpu.VMEM((nsub, 3 * slab, breadth), F32),
            pltpu.VMEM((ny, piece, breadth), F32),
            pltpu.VMEM((ny, piece, breadth), F32),
            pltpu.VMEM((piece, breadth), F32),
            pltpu.VMEM((nz, piece, breadth), F32),
            pltpu.VMEM((ny, piece, breadth), F32),
            signals((max(ny - 2, 2),)), signals((max(nz - 2, 2),)),
            dma((4,)),
            dma((CHUNKS,)), dma((CHUNKS,)), dma((CHUNKS,)), dma((CHUNKS,)),
            *[dma(())] * 18,
        ],
        compiler_params=pltpu.CompilerParams(
            collective_id=0, has_side_effects=True, vmem_limit_bytes=40 * 2**20
        ),
    )(hbm_only(operator), hbm_only(rhs), sizes, hbm_only(neighbours), hbm_only(kept))


BLOCK = 16


def update_kernel(
    live_ref, rounded_ref, image_ref, inverse_ref, rest_ref,
    solution_hbm, residual_hbm, direction_hbm,
    solution_ref, residual_ref, direction_ref, sems,
):
    nsub, rows3 = rest_ref.shape[:2]
    slab = rows3 // 3
    height = live_ref.shape[0]
    step = height // CHUNKS

    def matrix(k):
        return jnp.concatenate([rest_ref[s, k * slab : (k + 1) * slab, :] for s in range(nsub)], axis=0)

    inverse = inverse_ref[...]
    weights = dot(inverse, matrix(0), precision=HIGHEST)
    coupled = matrix(2) - dot(matrix(1), weights, precision=HIGHEST)
    correction = dot(inverse, coupled, precision=HIGHEST)
    wh, wm, wl = three_parts(weights)
    zh, zm, zl = three_parts(correction)
    n = weights.shape[0]
    wide = jnp.concatenate([wh, wm, wl, zh, zm, zl], axis=1)
    copies = []
    for t in range(CHUNKS):
        rows = pl.ds(t * step, step)
        live = live_ref[rows, :]
        spread = dot(rounded_ref[rows, :], wide)
        ih, im, il = three_parts(image_ref[rows, :])
        first = dot(ih, wide[:, : 3 * n])
        second = dot(im, wide[:, : 2 * n])
        third = dot(il, wh)
        moved = first[:, :n] + (first[:, n : 2 * n] + second[:, :n]) + (first[:, 2 * n :] + second[:, n:] + third)
        residual = live - moved
        solution_ref[rows, :] = spread[:, :n] + spread[:, n : 2 * n] + spread[:, 2 * n : 3 * n]
        residual_ref[rows, :] = residual
        direction_ref[rows, :] = residual - (
            spread[:, 3 * n : 4 * n] + spread[:, 4 * n : 5 * n] + spread[:, 5 * n :]
        )
        for k, (src, dst) in enumerate(
            [(solution_ref, solution_hbm), (residual_ref, residual_hbm), (direction_ref, direction_hbm)]
        ):
            copies.append(pltpu.make_async_copy(src.at[rows, :], dst.at[0, rows, :], sems.at[k, t]))
            copies[-1].start()
    for copy in copies:
        copy.wait()


def update(live, rounded, image, inverse, rest):
    vmem = pl.BlockSpec(memory_space=pltpu.VMEM)
    return pl.pallas_call(
        update_kernel,
        name="update",
        out_shape=[jax.ShapeDtypeStruct((1, *live.shape), F32)] * 3,
        in_specs=[vmem] * 5,
        out_specs=[pl.BlockSpec(memory_space=pltpu.HBM)] * 3,
        scratch_shapes=[pltpu.VMEM(live.shape, F32)] * 3 + [pltpu.SemaphoreType.DMA((3, CHUNKS))],
        compiler_params=pltpu.CompilerParams(vmem_limit_bytes=40 * 2**20),
    )(live, rounded, image, inverse, rest)


def per_device(ny, nz, nx, nc, operator, rhs, interface_sizes, neighbour_rows, kept_columns):
    results = communicate(operator, rhs, interface_sizes, neighbour_rows, kept_columns, ny, nz, nx, nc)
    return tuple(update(*results))


def solution(mesh, grid=(8, 12, 4, 2)):
    finer = Mesh(mesh.devices.reshape(grid), AXES)
    in_specs = (P(AXES, None, None), P(AXES, None, None), P(AXES), P(AXES, None), P())
    out_specs = (P(AXES, None, None),) * 3
    return jax.shard_map(
        functools.partial(per_device, *grid), mesh=finer, in_specs=in_specs, out_specs=out_specs, check_vma=False
    )
```
